32 devices in a mesh: feed: 8 (over y, x, core), tm: 4 (over z).
Axes of the slice: x: 2, y: 2, z: 4, core: 2. Of those that a mesh axis runs over, the one named last changes fastest.
Arguments:
- voltages: bfloat16 [256, 1048576], P('feed', 'tm'), may hold values from -12 to 12
- filter_taps: float32 [4, 1024], replicated, may hold values from -1 to 1
- delays: float32 [256], P('feed'), may hold values from -64 to 64
- channel_flags: int32 [512], P('feed'), may hold values from 0 to 1, as said below
Outputs:
- visibilities: float32 [512, 256, 256], P(('feed', 'tm'))
The draws below stay inside these ranges and needn't reach their ends.
Inputs may be any that keep to these rules, and one draw needn't show every extreme that they name: `channel_flags`: channel c belongs to owner c // 64; every owner keeps between 16 and 64 of its channels, and in every draw some owner keeps all of them.
All inputs are finite; a program needn't handle non-finite values.
Results may differ from the reference program's by a relative error of at most 0.0011.
Values may be sent and summed in bfloat16 or wider, within the bound.
A program may use at most 192 MiB of HBM per device.

```python
import math
import jax
import jax.numpy as jnp
from jax import lax

NI = 256
NFFT = 1024
TAPS = 4
SOURCES = 4
CHANNEL_COUNT = 512
S_TOT = 1024
CHANNELS_OWNED = 64


def draw_voltages(key, part):
    length = S_TOT * NFFT
    noise_key = jax.random.fold_in(key, 11)
    gain_key = jax.random.fold_in(key, 12)
    signal_key = jax.random.fold_in(key, 13)
    source_gains = jax.random.normal(gain_key, (NI, SOURCES), jnp.float32) * 0.5
    signals = jax.random.normal(signal_key, (SOURCES, length), jnp.float32)
    noise = jax.random.normal(noise_key, (NI, length), jnp.float32)
    result = noise
    for source in range(SOURCES):
        result = result + source_gains[:, source:source + 1] * signals[source][None, :]
    return jnp.clip(result, -12.0, 12.0).astype(jnp.bfloat16)


def draw_channel_flags(key, part):
    owner_total = CHANNEL_COUNT // CHANNELS_OWNED
    clean_channels = jax.random.randint(jax.random.fold_in(key, 21), (owner_total,), CHANNELS_OWNED // 4, CHANNELS_OWNED + 1)
    largest_owner_load = jax.random.randint(jax.random.fold_in(key, 22), (), 0, owner_total)
    clean_channels = jnp.where(jnp.arange(owner_total) == largest_owner_load, CHANNELS_OWNED, clean_channels)
    order_keys = jax.random.split(jax.random.fold_in(key, 23), owner_total)
    channel_orderings = jax.vmap(lambda order_key: jax.random.permutation(order_key, CHANNELS_OWNED))(order_keys)
    return (channel_orderings < clean_channels[:, None]).astype(jnp.int32).reshape(CHANNEL_COUNT)


def block_scale(key, shape, cuts, smallest, largest):
    def one(axis_at, blocks):
        steps = jax.random.uniform(jax.random.fold_in(jax.random.fold_in(key, 6), axis_at), (blocks,), jnp.float32, smallest / len(cuts), largest / len(cuts))
        return jnp.repeat(jnp.exp(steps), shape[axis_at] // blocks).reshape((-1,) + (1,) * (len(shape) - axis_at - 1))

    factor_of = one(*cuts[0])
    for cut in cuts[1:]:
        factor_of = factor_of * one(*cut)
    return factor_of


def setup_inputs(seed: int = 0) -> dict:
    key_of = jax.random.split(jax.random.key(seed), 5)
    voltages = draw_voltages(jax.random.fold_in(key_of[4], 71), 0)
    filter_taps = jnp.clip(jax.random.uniform(key_of[1], (TAPS, NFFT), jnp.float32, -1.0, 1.0), -1.0, 1.0)
    delays = jnp.clip(jax.random.uniform(key_of[2], (NI,), jnp.float32, -64.0, 64.0) * block_scale(key_of[2], (NI,), ((0, 8),), -0.4, 0.0), -64.0, 64.0)
    channel_flags = draw_channel_flags(jax.random.fold_in(key_of[4], 71), 0)
    return {"voltages": voltages, "filter_taps": filter_taps, "delays": delays, "channel_flags": channel_flags}


def build_table(fft_length):
    channels = jnp.arange(fft_length // 2, dtype=jnp.int32)
    samples = jnp.arange(fft_length, dtype=jnp.int32)
    product = channels[:, None] * samples[None, :] % fft_length
    angles = product.astype(jnp.float32) * (2.0 * math.pi / fft_length)
    return jnp.stack([jnp.cos(angles), -jnp.sin(angles)], axis=1).astype(jnp.bfloat16)

def rotate_phase(real_part, imag_part, channels, delay_values, fft_length):
    angles = 2.0 * math.pi / fft_length * channels * delay_values
    cosine = jnp.cos(angles)
    sine_part = jnp.sin(angles)
    factor = 1.0 / math.sqrt(fft_length)
    return ((real_part * cosine + imag_part * sine_part) * factor, (imag_part * cosine - real_part * sine_part) * factor)

def reference(voltages, filter_taps, delays, channel_flags):
    dft_table = build_table(NFFT).astype(jnp.float32)
    channels = jnp.arange(CHANNEL_COUNT).astype(jnp.float32)[:, None]

    def one_input(operands):
        samples, delay_value = operands
        frames = samples.reshape(S_TOT, NFFT).astype(jnp.float32)
        padded = jnp.concatenate([jnp.zeros((TAPS - 1, NFFT), jnp.float32), frames], axis=0)
        filtered = filter_taps[0] * padded[TAPS - 1:TAPS - 1 + S_TOT]
        for tap_index in range(1, TAPS):
            filtered = filtered + filter_taps[tap_index] * padded[TAPS - 1 - tap_index:TAPS - 1 - tap_index + S_TOT]
        filtered = lax.optimization_barrier(filtered.astype(jnp.bfloat16)).astype(jnp.float32)
        raw_spectra = jnp.einsum('cpn,sn->cps', dft_table, filtered, precision=lax.Precision.HIGHEST)
        real_part, imag_part = rotate_phase(raw_spectra[:, 0], raw_spectra[:, 1], channels, delay_value, NFFT)
        return jnp.stack([real_part, imag_part], axis=1).astype(jnp.bfloat16)
    spectra = lax.map(one_input, (voltages, delays))
    upper_mask = jnp.arange(NI)[:, None] <= jnp.arange(NI)[None, :]

    def one_channel(channel_index):
        channel_slab = lax.dynamic_index_in_dim(spectra, channel_index, axis=1, keepdims=False)
        direct = channel_slab.reshape(NI, 2 * S_TOT).astype(jnp.float32)
        swapped = jnp.concatenate([channel_slab[:, 1], -channel_slab[:, 0]], axis=1).astype(jnp.float32)
        real_gram = jnp.dot(direct, direct.T, precision=lax.Precision.HIGHEST)
        imag_gram = jnp.dot(swapped, direct.T, precision=lax.Precision.HIGHEST)
        packed = jnp.where(upper_mask, real_gram, imag_gram) / S_TOT
        flag_value = lax.dynamic_index_in_dim(channel_flags, channel_index, keepdims=False)
        return packed * flag_value.astype(jnp.float32)
    return lax.map(one_channel, jnp.arange(CHANNEL_COUNT, dtype=jnp.int32))
```

```python
import functools
import math

import jax
import jax.numpy as jnp
import numpy as np
from jax import lax
from jax.experimental import pallas as pl
from jax.experimental.pallas import tpu as pltpu
from jax.sharding import PartitionSpec as P

VMEM_LIMIT = 56 * 1024 * 1024
SEND_PEAK = 16384.0
EXTRA_ROWS = 8


def passed_along(block, axis, distance):
    devices = range(lax.axis_size(axis))
    route = [(i - distance, i) for i in devices if i - distance in devices]
    return lax.ppermute(block, axis, route)


def table_rows(channels, fft_length):
    samples = np.arange(fft_length, dtype=np.int64)
    product = channels[:, None].astype(np.int64) * samples[None, :] % fft_length
    angles = product.astype(np.float32) * np.float32(2.0 * math.pi / fft_length)
    rows = np.concatenate([np.cos(angles), -np.sin(angles)], axis=0)
    return rows.astype(jnp.bfloat16)


def dft_kernel(table_ref, cos_ref, sin_ref, filtered_ref, out_ref, *turned):
    inputs, frames = filtered_ref.shape[0], filtered_ref.shape[1]
    rows = table_ref.shape[0] // 2
    width = 128
    for i in range(inputs):
        raw = lax.dot_general(
            table_ref[...], filtered_ref[i], (((1,), (1,)), ((), ())),
            preferred_element_type=jnp.float32,
        )
        real, imag = raw[:rows], raw[rows:]
        cosine = cos_ref[0, :, i : i + 1]
        sine = sin_ref[0, :, i : i + 1]
        both = (real * cosine + imag * sine, imag * cosine - real * sine)
        for q in range(2):
            for piece in range(frames // width):
                turned[q * (frames // width) + piece][pl.ds(i, rows, stride=inputs), :] = both[q][
                    :, piece * width : (piece + 1) * width
                ]
    for piece, ref in enumerate(turned):
        value = ref[...].reshape(rows, inputs, width).astype(jnp.bfloat16)
        out_ref[:, :, piece * width : (piece + 1) * width] = value


def dft_call(table, cosine, sine, filtered):
    blocks, rows, inputs = cosine.shape
    inputs_here, frames, fft_length = filtered.shape
    out_shape = jax.ShapeDtypeStruct((rows, inputs_here, 2 * frames), jnp.bfloat16)
    return pl.pallas_call(
        dft_kernel,
        out_shape=out_shape,
        grid=(blocks,),
        in_specs=[
            pl.BlockSpec((2 * rows, fft_length), lambda b: (0, 0)),
            pl.BlockSpec((1, rows, inputs), lambda b: (b, 0, 0)),
            pl.BlockSpec((1, rows, inputs), lambda b: (b, 0, 0)),
            pl.BlockSpec((inputs, frames, fft_length), lambda b: (b, 0, 0)),
        ],
        out_specs=pl.BlockSpec((rows, inputs, 2 * frames), lambda b: (0, b, 0)),
        scratch_shapes=[pltpu.VMEM((rows * inputs, 128), jnp.float32)] * (2 * frames // 128),
        compiler_params=pltpu.CompilerParams(vmem_limit_bytes=VMEM_LIMIT),
        cost_estimate=pl.CostEstimate(
            flops=10 * 4 * rows * inputs_here * frames * fft_length,
            bytes_accessed=2 * inputs_here * frames * (fft_length + 2 * rows),
            transcendentals=0,
        ),
    )(table, cosine, sine, filtered)


def gram_kernel(spectra_ref, vis_ref):
    sources, channels, inputs_here, columns = spectra_ref.shape
    total = sources * inputs_here
    half = columns // 2
    row = lax.broadcasted_iota(jnp.int32, (total, total), 0)
    column = lax.broadcasted_iota(jnp.int32, (total, total), 1)
    dims = (((1,), (1,)), ((), ()))
    for c in range(channels):
        slab = spectra_ref[:, c]
        if inputs_here % 16:
            slab = slab.astype(jnp.float32).reshape(total, columns).astype(jnp.bfloat16)
        else:
            slab = slab.reshape(total, columns)
        swapped = jnp.concatenate([slab[:, half:], -slab[:, :half]], axis=1)
        real = lax.dot_general(slab, slab, dims, preferred_element_type=jnp.float32)
        imag = lax.dot_general(swapped, slab, dims, preferred_element_type=jnp.float32)
        packed = jnp.where(row <= column, real, imag)
        peak = jnp.max(jnp.where(row == column, real, 0.0), axis=(0, 1), keepdims=True)
        peak = jnp.maximum(peak, 1e-30)
        power = jnp.ceil(jnp.log2(peak))
        vis_ref[c, :total] = packed * (SEND_PEAK * jnp.exp2(-power))
        vis_ref[c, total:] = jnp.broadcast_to(power, (EXTRA_ROWS, total))


def gram_call(spectra):
    sources, channels, inputs_here, columns = spectra.shape
    total = sources * inputs_here
    step = 2 if channels % 2 == 0 else 1
    return pl.pallas_call(
        gram_kernel,
        out_shape=jax.ShapeDtypeStruct((channels, total + EXTRA_ROWS, total), jnp.float32),
        grid=(channels // step,),
        in_specs=[pl.BlockSpec((sources, step, inputs_here, columns), lambda b: (0, b, 0, 0))],
        out_specs=pl.BlockSpec((step, total + EXTRA_ROWS, total), lambda b: (b, 0, 0)),
        compiler_params=pltpu.CompilerParams(vmem_limit_bytes=VMEM_LIMIT),
        cost_estimate=pl.CostEstimate(
            flops=40 * 4 * channels * total * total * columns,
            bytes_accessed=2 * channels * total * (columns + 2 * total),
            transcendentals=0,
        ),
    )(spectra)


def filter_kernel(history_ref, taps_ref, block_ref, out_ref, carry, turned):
    tap_count, fft_length = taps_ref.shape
    inputs, group = out_ref.shape[0], out_ref.shape[1]
    kept = tap_count - 1

    @pl.when(pl.program_id(0) == 0)
    def _():
        carry[...] = history_ref[...]

    def piece(p, unused):
        lanes = pl.multiple_of(p * 128, 128)
        taps = [taps_ref[t : t + 1, pl.ds(lanes, 128)] for t in range(tap_count)]
        frames = [
            carry[:, pl.ds(pl.multiple_of(h * fft_length + lanes, 128), 128)].astype(jnp.float32)
            for h in range(kept)
        ]
        for m in range(group):
            start = pl.multiple_of(m * fft_length + lanes, 128)
            frames.append(block_ref[:, pl.ds(start, 128)].astype(jnp.float32))
            value = taps[0] * frames[-1]
            for t in range(1, tap_count):
                value = value + taps[t] * frames[-1 - t]
            turned[pl.ds(m, inputs, stride=group), :] = value
        result = turned[...].reshape(inputs, group, 128).astype(jnp.bfloat16)
        out_ref[:, :, pl.ds(lanes, 128)] = result
        return unused

    lax.fori_loop(0, fft_length // 128, piece, 0)
    carry[...] = block_ref[:, (group - kept) * fft_length :]


def filter_frames(voltages, filter_taps):
    inputs_here, sample_count = voltages.shape
    tap_count, fft_length = filter_taps.shape
    frames = sample_count // fft_length
    kept = (tap_count - 1) * fft_length
    group = 16
    history = passed_along(voltages[:, sample_count - kept :], "tm", 1)
    return pl.pallas_call(
        filter_kernel,
        out_shape=jax.ShapeDtypeStruct((inputs_here, frames, fft_length), jnp.bfloat16),
        grid=(frames // group,),
        in_specs=[
            pl.BlockSpec((inputs_here, kept), lambda b: (0, 0)),
            pl.BlockSpec((tap_count, fft_length), lambda b: (0, 0)),
            pl.BlockSpec((inputs_here, group * fft_length), lambda b: (0, b)),
        ],
        out_specs=pl.BlockSpec((inputs_here, group, fft_length), lambda b: (0, b, 0)),
        scratch_shapes=[
            pltpu.VMEM((inputs_here, kept), jnp.bfloat16),
            pltpu.VMEM((inputs_here * group, 128), jnp.float32),
        ],
        compiler_params=pltpu.CompilerParams(vmem_limit_bytes=VMEM_LIMIT),
        cost_estimate=pl.CostEstimate(
            flops=8 * inputs_here * sample_count,
            bytes_accessed=4 * inputs_here * sample_count,
            transcendentals=0,
        ),
    )(history, filter_taps, voltages)


def on_device_steps(voltages, filter_taps, delays, channel_flags):
    inputs_here = voltages.shape[0]
    fft_length = filter_taps.shape[1]
    feeds, times = lax.axis_size("feed"), lax.axis_size("tm")
    filtered = filter_frames(voltages, filter_taps)
    frame_total = filtered.shape[1] * times
    owned = channel_flags.shape[0]
    kept = owned // times
    chunks = 4 if kept % 4 == 0 else 1
    width = kept // chunks
    block = 16 if inputs_here % 16 == 0 else inputs_here

    local_flags = lax.dynamic_slice_in_dim(
        channel_flags, lax.axis_index("tm") * kept, kept, 0
    ).astype(jnp.float32)
    flag_parts = (local_flags * (1.0 / (SEND_PEAK * frame_total))).reshape(chunks, width)
    scale = 1.0 / math.sqrt(fft_length)
    order = np.arange(feeds * owned).reshape(feeds, times, chunks, width)
    place = lax.axis_index("tm")

    def summed(vis, flags):
        total = 0.0
        for shift in range(times):
            target = lax.rem(place + shift, times)
            part = lax.dynamic_index_in_dim(vis, target, 0, keepdims=False)
            if shift:
                route = [(i, (i + shift) % times) for i in range(times)]
                part = lax.ppermute(part, "tm", route)
            part = part.astype(jnp.float32)
            count = part.shape[2]
            total = total + part[:, :count] * jnp.exp2(part[:, count:, :1][:, :1])
        return total * flags[:, None, None]

    results = []
    sent = []
    for k in range(chunks):
        channels = order[:, :, k].reshape(-1)
        table = jnp.asarray(table_rows(channels, fft_length))
        angles = 2.0 * math.pi / fft_length * jnp.asarray(channels, jnp.float32)[None, :, None]
        angles = angles * delays.reshape(-1, 1, block)
        if k >= 2:
            filtered, sent[k - 2] = lax.optimization_barrier((filtered, sent[k - 2]))
            results.append(summed(sent[k - 2], flag_parts[k - 2]))
        spectra = dft_call(table, jnp.cos(angles) * scale, jnp.sin(angles) * scale, filtered)
        spectra = spectra.reshape(feeds, times * width, inputs_here, spectra.shape[2])
        if k >= 3:
            spectra, results[k - 3] = lax.optimization_barrier((spectra, results[k - 3]))
        turned = lax.all_to_all(spectra, "feed", split_axis=0, concat_axis=0, tiled=True)
        if k >= 2:
            turned, results[k - 2] = lax.optimization_barrier((turned, results[k - 2]))
        vis = gram_call(turned).astype(jnp.float16)
        sent.append(vis.reshape(times, width, vis.shape[1], vis.shape[2]))
    for k in range(len(results), chunks):
        results.append(summed(sent[k], flag_parts[k]))
    return jnp.concatenate(results, axis=0)


VMEM_WHOLE = 63 * 1000 * 1000
MESH = pl.DeviceIdType.MESH
HALF = 16
GROUP = 16
UNITS = 4
LEVELS = 32760.0
NOTE_ROWS = 16
RING = 4


def whole_kernel(
    volt_ref, taps_ref, table_ref, cos_ref, sin_ref, out_ref,
    stage, history, filtered, turned, send, recv, own, zsend, zrecv,
    stage_sem, history_sems, send_sem, recv_sem, self_sem, zsend_sem, zrecv_sem, out_sem,
):
    feeds, times = lax.axis_size("feed"), lax.axis_size("tm")
    me, place = lax.axis_index("feed"), lax.axis_index("tm")
    inputs, sample_count = volt_ref.shape
    tap_count, fft_length = taps_ref.shape
    frames = sample_count // fft_length
    kept = tap_count - 1
    groups = frames // GROUP
    halves = inputs // HALF
    chunks = table_ref.shape[0]
    rows = table_ref.shape[1] // 2
    unit_count = chunks * UNITS
    total = feeds * inputs
    width = 128
    pieces = 2 * frames // width

    barrier = pltpu.get_barrier_semaphore()
    for s in range(1, feeds):
        pl.semaphore_signal(barrier, inc=1, device_id=(me ^ s, place), device_id_type=MESH)
    for s in range(1, times):
        other = lax.rem(place + s, times)
        pl.semaphore_signal(barrier, inc=1, device_id=(me, other), device_id_type=MESH)
    pl.semaphore_wait(barrier, feeds + times - 2)

    def history_copy():
        return pltpu.make_async_remote_copy(
            src_ref=volt_ref.at[:, pl.ds(sample_count - kept * fft_length, kept * fft_length)],
            dst_ref=history,
            send_sem=history_sems.at[0],
            recv_sem=history_sems.at[1],
            device_id=(me, place + 1),
            device_id_type=MESH,
        )

    @pl.when(place < times - 1)
    def _():
        history_copy().start()

    def block_copies(h, step):
        g = lax.rem(step + 1, groups)
        slot = lax.rem(step, 2)
        at = pl.ds(pl.multiple_of(h * HALF, HALF), HALF)
        first = pl.multiple_of(jnp.maximum(g * GROUP - kept, 0) * fft_length, 128)
        later = pltpu.make_async_copy(
            volt_ref.at[at, pl.ds(first, (GROUP + kept) * fft_length)],
            stage.at[slot],
            stage_sem.at[slot],
        )
        start = pltpu.make_async_copy(
            volt_ref.at[at, pl.ds(0, GROUP * fft_length)],
            stage.at[slot, :, pl.ds(kept * fft_length, GROUP * fft_length)],
            stage_sem.at[slot],
        )
        return g, slot, later, start

    def block_start(h, step):
        g, _, later, start = block_copies(h, step)

        @pl.when(g > 0)
        def _():
            later.start()

        @pl.when(g == 0)
        def _():
            start.start()

    def filter_half(h):
        block_start(h, 0)

        def step_body(step, unused):
            @pl.when(step + 1 < groups)
            def _():
                block_start(h, step + 1)

            g, slot, later, start = block_copies(h, step)

            @pl.when(g > 0)
            def _():
                later.wait()

            @pl.when(g == 0)
            def _():
                start.wait()

                @pl.when(place == 0)
                def _():
                    stage[slot, :, : kept * fft_length] = jnp.zeros(
                        (HALF, kept * fft_length), jnp.bfloat16
                    )

                @pl.when(place > 0)
                def _():
                    @pl.when(h == 0)
                    def _():
                        history_copy().wait_recv()

                    at = pl.ds(pl.multiple_of(h * HALF, HALF), HALF)
                    stage[slot, :, : kept * fft_length] = history[at, :]

            def piece(p, unused):
                lanes = pl.multiple_of(p * 128, 128)
                taps = [taps_ref[t : t + 1, pl.ds(lanes, 128)] for t in range(tap_count)]

                def frame(j):
                    column = pl.multiple_of(j * fft_length + lanes, 128)
                    return stage[slot, :, pl.ds(column, 128)].astype(jnp.float32)

                window = [frame(j) for j in range(kept)]
                for m in range(GROUP):
                    window.append(frame(m + kept))
                    value = taps[0] * window[-1]
                    for t in range(1, tap_count):
                        value = value + taps[t] * window[-1 - t]
                    turned[0, pl.ds(m, HALF, stride=GROUP), :] = value
                result = turned[0, : HALF * GROUP].reshape(HALF, GROUP, 128).astype(jnp.bfloat16)
                at = pl.ds(pl.multiple_of(h * HALF, HALF), HALF)
                of = pl.ds(pl.multiple_of(g * GROUP, GROUP), GROUP)
                filtered[at, of, pl.ds(lanes, 128)] = result
                return unused

            return lax.fori_loop(0, fft_length // 128, piece, unused)

        lax.fori_loop(0, groups, step_body, 0)

    def transform(k, h):
        slot = lax.rem(k, 2)
        cosine_all = jnp.transpose(cos_ref[k, h])
        sine_all = jnp.transpose(sin_ref[k, h])
        for i in range(HALF):
            raw = lax.dot_general(
                table_ref[k], filtered[h * HALF + i], (((1,), (1,)), ((), ())),
                preferred_element_type=jnp.float32,
            )
            real, imag = raw[:rows], raw[rows:]
            cosine = cosine_all[:, i : i + 1]
            sine = sine_all[:, i : i + 1]
            both = (real * cosine + imag * sine, imag * cosine - real * sine)
            for q in range(2):
                for part in range(frames // width):
                    turned[q * (frames // width) + part, pl.ds(i, rows, stride=HALF), :] = both[q][
                        :, part * width : (part + 1) * width
                    ]
        at = pl.ds(pl.multiple_of(h * HALF, HALF), HALF)
        for part in range(pieces):
            value = turned[part].reshape(rows, HALF, width).astype(jnp.bfloat16)
            send[slot, :, at, part * width : (part + 1) * width] = value

    def unit_copies(k, u, at):
        slot = lax.rem(k, 2)
        g = k * UNITS + u
        copies = []
        for s in range(1, feeds):
            peer = me ^ s
            copies.append(
                pltpu.make_async_remote_copy(
                    src_ref=send.at[slot, pl.ds((u * feeds + peer) * times, times), at],
                    dst_ref=recv.at[g, me, :, at],
                    send_sem=send_sem.at[g, s],
                    recv_sem=recv_sem.at[g, s],
                    device_id=(peer, place),
                    device_id_type=MESH,
                )
            )
        mine = pltpu.make_async_copy(
            send.at[slot, pl.ds((u * feeds + me) * times, times), at],
            recv.at[g, me, :, at],
            self_sem.at[g],
        )
        return copies, mine

    def send_units(k, at):
        def one(u, unused):
            copies, mine = unit_copies(k, u, at)
            for copy in copies:
                copy.start()
            mine.start()
            return unused

        lax.fori_loop(0, UNITS, one, 0)

    whole = pl.ds(0, inputs)

    def sent_units(k):
        def one(u, unused):
            copies, _ = unit_copies(k, u, whole)
            for copy in copies:
                copy.wait_send()
            return unused

        lax.fori_loop(0, UNITS, one, 0)

    row = lax.broadcasted_iota(jnp.int32, (total, total), 0)
    column = lax.broadcasted_iota(jnp.int32, (total, total), 1)
    dims = (((1,), (1,)), ((), ()))

    def zcopy(g, s):
        slot = lax.rem(g, RING)
        return pltpu.make_async_remote_copy(
            src_ref=zsend.at[slot, s - 1],
            dst_ref=zrecv.at[g, s - 1],
            send_sem=zsend_sem.at[g, s],
            recv_sem=zrecv_sem.at[g, s],
            device_id=(me, lax.rem(place + s, times)),
            device_id_type=MESH,
        )

    def out_copy(g):
        slot = lax.rem(g, RING)
        return pltpu.make_async_copy(own.at[slot], out_ref.at[g], out_sem.at[slot])

    def gram(g):
        k, u = g // UNITS, lax.rem(g, UNITS)
        copies, mine = unit_copies(k, u, whole)
        for copy in copies:
            copy.wait_recv()
        mine.wait()
        slot = lax.rem(g, RING)

        @pl.when(g >= RING)
        def _():
            for s in range(1, times):
                zcopy(g - RING, s).wait_send()
            out_copy(g - RING).wait()

        for s in list(range(1, times)) + [0]:
            target = lax.rem(place + s, times)
            slab = recv[g, :, target].reshape(total, 2 * frames)
            swapped = jnp.concatenate([slab[:, frames:], -slab[:, :frames]], axis=1)
            real = lax.dot_general(slab, slab, dims, preferred_element_type=jnp.float32)
            imag = lax.dot_general(swapped, slab, dims, preferred_element_type=jnp.float32)
            packed = jnp.where(row <= column, real, imag)
            if s == 0:
                own[slot] = packed
                continue
            diagonal = jnp.where(row == column, real, 0.0)
            powers = [
                jnp.ceil(0.5 * jnp.log2(jnp.maximum(jnp.sum(diagonal, axis=a, keepdims=True), 1e-30)))
                for a in range(2)
            ]
            scaled = packed * (LEVELS * jnp.exp2(-powers[0])) * jnp.exp2(-powers[1])
            zsend[slot, s - 1, :total] = jnp.round(scaled).astype(jnp.int32).astype(jnp.int16)
            note = jnp.broadcast_to(powers[0], (NOTE_ROWS, total))
            zsend[slot, s - 1, total:] = note.astype(jnp.int32).astype(jnp.int16)
            zcopy(g, s).start()

    def finish(g):
        slot = lax.rem(g, RING)
        result = own[slot]
        for s in range(1, times):
            zcopy(g, s).wait_recv()
            value = zrecv[g, s - 1, :total].astype(jnp.int32).astype(jnp.float32)
            across = jnp.exp2(zrecv[g, s - 1, total:].astype(jnp.int32).astype(jnp.float32))[:1]
            down = jnp.sum(jnp.where(row == column, across, 0.0), axis=1, keepdims=True)
            result = result + value * across * (down * (1.0 / LEVELS))
        own[slot] = result
        out_copy(g).start()

    def head(h, unused):
        filter_half(h)
        transform(0, h)
        send_units(0, pl.ds(pl.multiple_of(h * HALF, HALF), HALF))
        return unused

    lax.fori_loop(0, halves, head, 0)

    lag = RING - 1

    def units_of(k):
        def one(u, unused):
            g = k * UNITS + u
            gram(g)

            @pl.when(g >= lag)
            def _():
                finish(g - lag)

            return unused

        lax.fori_loop(0, UNITS, one, 0)

    def main(k, unused):
        @pl.when(k < chunks)
        def _():
            @pl.when(k >= 2)
            def _():
                sent_units(k - 2)

            def half(h, unused):
                transform(k, h)
                return unused

            lax.fori_loop(0, halves, half, 0)
            send_units(k, whole)

        units_of(k - 1)
        return unused

    lax.fori_loop(1, chunks + 1, main, 0)

    def last(j, unused):
        finish(unit_count - lag + j)
        return unused

    lax.fori_loop(0, lag, last, 0)

    for k in range(max(chunks - 2, 0), chunks):
        sent_units(k)

    def drain(j, unused):
        g = unit_count - RING + j
        for s in range(1, times):
            zcopy(g, s).wait_send()
        out_copy(g).wait()
        return unused

    lax.fori_loop(0, RING, drain, 0)

    @pl.when(place < times - 1)
    def _():
        history_copy().wait_send()


def whole_call(voltages, filter_taps, table, cosine, sine):
    feeds, times = lax.axis_size("feed"), lax.axis_size("tm")
    inputs, sample_count = voltages.shape
    tap_count, fft_length = filter_taps.shape
    frames = sample_count // fft_length
    chunks, rows = table.shape[0], table.shape[1] // 2
    units = chunks * UNITS
    total = feeds * inputs
    kept = tap_count - 1
    vmem = pl.BlockSpec(memory_space=pltpu.VMEM)
    return pl.pallas_call(
        whole_kernel,
        out_shape=jax.ShapeDtypeStruct((units, total, total), jnp.float32),
        in_specs=[pl.BlockSpec(memory_space=pl.ANY), vmem, vmem, vmem, vmem],
        out_specs=pl.BlockSpec(memory_space=pl.ANY),
        scratch_shapes=[
            pltpu.VMEM((2, HALF, (GROUP + kept) * fft_length), jnp.bfloat16),
            pltpu.VMEM((inputs, kept * fft_length), jnp.bfloat16),
            pltpu.VMEM((inputs, frames, fft_length), jnp.bfloat16),
            pltpu.VMEM((2 * frames // 128, rows * HALF, 128), jnp.float32),
            pltpu.VMEM((2, rows, inputs, 2 * frames), jnp.bfloat16),
            pltpu.VMEM((units, feeds, times, inputs, 2 * frames), jnp.bfloat16),
            pltpu.VMEM((RING, total, total), jnp.float32),
            pltpu.VMEM((RING, times - 1, total + NOTE_ROWS, total), jnp.int16),
            pltpu.VMEM((units, times - 1, total + NOTE_ROWS, total), jnp.int16),
            pltpu.SemaphoreType.DMA((2,)),
            pltpu.SemaphoreType.DMA((2,)),
            pltpu.SemaphoreType.DMA((units, feeds)),
            pltpu.SemaphoreType.DMA((units, feeds)),
            pltpu.SemaphoreType.DMA((units,)),
            pltpu.SemaphoreType.DMA((units, times)),
            pltpu.SemaphoreType.DMA((units, times)),
            pltpu.SemaphoreType.DMA((RING,)),
        ],
        compiler_params=pltpu.CompilerParams(
            vmem_limit_bytes=VMEM_WHOLE, collective_id=0, has_side_effects=True
        ),
        cost_estimate=pl.CostEstimate(
            flops=8 * inputs * sample_count * 512,
            bytes_accessed=4 * inputs * sample_count,
            transcendentals=0,
        ),
    )(voltages, filter_taps, table, cosine, sine)


def whole_fits(voltages, filter_taps, channel_flags, feeds, times):
    inputs, frames = voltages.shape[0], voltages.shape[1] // filter_taps.shape[1]
    kept = channel_flags.shape[0] // times
    rows = UNITS * feeds * times
    if inputs % HALF or feeds & (feeds - 1) or kept % UNITS or frames % 128:
        return False
    if kept < 2 * UNITS or frames < 2 * GROUP:
        return False
    spectra = 2 * inputs * 2 * frames
    total = feeds * inputs
    held = 2 * inputs * voltages.shape[1]
    held += spectra * (2 * rows + kept * feeds * times) + 8 * frames * rows * HALF
    held += 2 * (RING + kept) * (times - 1) * (total + NOTE_ROWS) * total + 4 * RING * total * total
    return held < VMEM_WHOLE - 4 * 1000 * 1000


def on_device_whole(voltages, filter_taps, delays, channel_flags):
    inputs = voltages.shape[0]
    fft_length = filter_taps.shape[1]
    feeds, times = lax.axis_size("feed"), lax.axis_size("tm")
    frame_total = voltages.shape[1] // fft_length * times
    owned = channel_flags.shape[0]
    kept = owned // times
    chunks = kept // UNITS
    order = np.arange(feeds * owned).reshape(feeds, times, chunks, UNITS)
    order = order.transpose(2, 3, 0, 1).reshape(chunks, -1)
    table = jnp.asarray(np.stack([table_rows(order[k], fft_length) for k in range(chunks)]))
    angles = 2.0 * math.pi / fft_length * jnp.asarray(order, jnp.float32)[:, None, :]
    angles = angles * delays[None, :, None]
    scale = 1.0 / math.sqrt(fft_length)
    shape = (chunks, inputs // HALF, HALF, order.shape[1])
    cosine = (jnp.cos(angles) * scale).reshape(shape)
    sine = (jnp.sin(angles) * scale).reshape(shape)
    vis = whole_call(voltages, filter_taps, table, cosine, sine)
    flags = lax.dynamic_slice_in_dim(channel_flags, lax.axis_index("tm") * kept, kept, 0)
    return vis * (flags.astype(jnp.float32) * (1.0 / frame_total))[:, None, None]


def on_device(voltages, filter_taps, delays, channel_flags):
    feeds, times = lax.axis_size("feed"), lax.axis_size("tm")
    if whole_fits(voltages, filter_taps, channel_flags, feeds, times):
        return on_device_whole(voltages, filter_taps, delays, channel_flags)
    return on_device_steps(voltages, filter_taps, delays, channel_flags)


def solution(mesh):
    in_specs = (P("feed", "tm"), P(), P("feed"), P("feed"))
    out_specs = P(("feed", "tm"), None, None)
    return jax.shard_map(
        on_device, mesh=mesh, in_specs=in_specs, out_specs=out_specs, check_vma=False
    )
```

```python
import functools
import math

import jax
import jax.numpy as jnp
import numpy as np
from jax import lax
from jax.experimental import pallas as pl
from jax.experimental.pallas import tpu as pltpu
from jax.sharding import PartitionSpec as P

VMEM_LIMIT = 56 * 1024 * 1024
SEND_PEAK = 16384.0
EXTRA_ROWS = 8


def passed_along(block, axis, distance):
    devices = range(lax.axis_size(axis))
    route = [(i - distance, i) for i in devices if i - distance in devices]
    return lax.ppermute(block, axis, route)


def table_rows(channels, fft_length):
    samples = np.arange(fft_length, dtype=np.int64)
    product = channels[:, None].astype(np.int64) * samples[None, :] % fft_length
    angles = product.astype(np.float32) * np.float32(2.0 * math.pi / fft_length)
    rows = np.concatenate([np.cos(angles), -np.sin(angles)], axis=0)
    return rows.astype(jnp.bfloat16)


def dft_kernel(table_ref, cos_ref, sin_ref, filtered_ref, out_ref, *turned):
    inputs, frames = filtered_ref.shape[0], filtered_ref.shape[1]
    rows = table_ref.shape[0] // 2
    width = 128
    for i in range(inputs):
        raw = lax.dot_general(
            table_ref[...], filtered_ref[i], (((1,), (1,)), ((), ())),
            preferred_element_type=jnp.float32,
        )
        real, imag = raw[:rows], raw[rows:]
        cosine = cos_ref[0, :, i : i + 1]
        sine = sin_ref[0, :, i : i + 1]
        both = (real * cosine + imag * sine, imag * cosine - real * sine)
        for q in range(2):
            for piece in range(frames // width):
                turned[q * (frames // width) + piece][pl.ds(i, rows, stride=inputs), :] = both[q][
                    :, piece * width : (piece + 1) * width
                ]
    for piece, ref in enumerate(turned):
        value = ref[...].reshape(rows, inputs, width).astype(jnp.bfloat16)
        out_ref[:, :, piece * width : (piece + 1) * width] = value


def dft_call(table, cosine, sine, filtered):
    blocks, rows, inputs = cosine.shape
    inputs_here, frames, fft_length = filtered.shape
    out_shape = jax.ShapeDtypeStruct((rows, inputs_here, 2 * frames), jnp.bfloat16)
    return pl.pallas_call(
        dft_kernel,
        out_shape=out_shape,
        grid=(blocks,),
        in_specs=[
            pl.BlockSpec((2 * rows, fft_length), lambda b: (0, 0)),
            pl.BlockSpec((1, rows, inputs), lambda b: (b, 0, 0)),
            pl.BlockSpec((1, rows, inputs), lambda b: (b, 0, 0)),
            pl.BlockSpec((inputs, frames, fft_length), lambda b: (b, 0, 0)),
        ],
        out_specs=pl.BlockSpec((rows, inputs, 2 * frames), lambda b: (0, b, 0)),
        scratch_shapes=[pltpu.VMEM((rows * inputs, 128), jnp.float32)] * (2 * frames // 128),
        compiler_params=pltpu.CompilerParams(vmem_limit_bytes=VMEM_LIMIT),
        cost_estimate=pl.CostEstimate(
            flops=10 * 4 * rows * inputs_here * frames * fft_length,
            bytes_accessed=2 * inputs_here * frames * (fft_length + 2 * rows),
            transcendentals=0,
        ),
    )(table, cosine, sine, filtered)


def gram_kernel(spectra_ref, vis_ref):
    sources, channels, inputs_here, columns = spectra_ref.shape
    total = sources * inputs_here
    half = columns // 2
    row = lax.broadcasted_iota(jnp.int32, (total, total), 0)
    column = lax.broadcasted_iota(jnp.int32, (total, total), 1)
    dims = (((1,), (1,)), ((), ()))
    for c in range(channels):
        slab = spectra_ref[:, c]
        if inputs_here % 16:
            slab = slab.astype(jnp.float32).reshape(total, columns).astype(jnp.bfloat16)
        else:
            slab = slab.reshape(total, columns)
        swapped = jnp.concatenate([slab[:, half:], -slab[:, :half]], axis=1)
        real = lax.dot_general(slab, slab, dims, preferred_element_type=jnp.float32)
        imag = lax.dot_general(swapped, slab, dims, preferred_element_type=jnp.float32)
        packed = jnp.where(row <= column, real, imag)
        peak = jnp.max(jnp.where(row == column, real, 0.0), axis=(0, 1), keepdims=True)
        peak = jnp.maximum(peak, 1e-30)
        power = jnp.ceil(jnp.log2(peak))
        vis_ref[c, :total] = packed * (SEND_PEAK * jnp.exp2(-power))
        vis_ref[c, total:] = jnp.broadcast_to(power, (EXTRA_ROWS, total))


def gram_call(spectra):
    sources, channels, inputs_here, columns = spectra.shape
    total = sources * inputs_here
    step = 2 if channels % 2 == 0 else 1
    return pl.pallas_call(
        gram_kernel,
        out_shape=jax.ShapeDtypeStruct((channels, total + EXTRA_ROWS, total), jnp.float32),
        grid=(channels // step,),
        in_specs=[pl.BlockSpec((sources, step, inputs_here, columns), lambda b: (0, b, 0, 0))],
        out_specs=pl.BlockSpec((step, total + EXTRA_ROWS, total), lambda b: (b, 0, 0)),
        compiler_params=pltpu.CompilerParams(vmem_limit_bytes=VMEM_LIMIT),
        cost_estimate=pl.CostEstimate(
            flops=40 * 4 * channels * total * total * columns,
            bytes_accessed=2 * channels * total * (columns + 2 * total),
            transcendentals=0,
        ),
    )(spectra)


def filter_kernel(history_ref, taps_ref, block_ref, out_ref, carry, turned):
    tap_count, fft_length = taps_ref.shape
    inputs, group = out_ref.shape[0], out_ref.shape[1]
    kept = tap_count - 1

    @pl.when(pl.program_id(0) == 0)
    def _():
        carry[...] = history_ref[...]

    def piece(p, unused):
        lanes = pl.multiple_of(p * 128, 128)
        taps = [taps_ref[t : t + 1, pl.ds(lanes, 128)] for t in range(tap_count)]
        frames = [
            carry[:, pl.ds(pl.multiple_of(h * fft_length + lanes, 128), 128)].astype(jnp.float32)
            for h in range(kept)
        ]
        for m in range(group):
            start = pl.multiple_of(m * fft_length + lanes, 128)
            frames.append(block_ref[:, pl.ds(start, 128)].astype(jnp.float32))
            value = taps[0] * frames[-1]
            for t in range(1, tap_count):
                value = value + taps[t] * frames[-1 - t]
            turned[pl.ds(m, inputs, stride=group), :] = value
        result = turned[...].reshape(inputs, group, 128).astype(jnp.bfloat16)
        out_ref[:, :, pl.ds(lanes, 128)] = result
        return unused

    lax.fori_loop(0, fft_length // 128, piece, 0)
    carry[...] = block_ref[:, (group - kept) * fft_length :]


def filter_frames(voltages, filter_taps):
    inputs_here, sample_count = voltages.shape
    tap_count, fft_length = filter_taps.shape
    frames = sample_count // fft_length
    kept = (tap_count - 1) * fft_length
    group = 16
    history = passed_along(voltages[:, sample_count - kept :], "tm", 1)
    return pl.pallas_call(
        filter_kernel,
        out_shape=jax.ShapeDtypeStruct((inputs_here, frames, fft_length), jnp.bfloat16),
        grid=(frames // group,),
        in_specs=[
            pl.BlockSpec((inputs_here, kept), lambda b: (0, 0)),
            pl.BlockSpec((tap_count, fft_length), lambda b: (0, 0)),
            pl.BlockSpec((inputs_here, group * fft_length), lambda b: (0, b)),
        ],
        out_specs=pl.BlockSpec((inputs_here, group, fft_length), lambda b: (0, b, 0)),
        scratch_shapes=[
            pltpu.VMEM((inputs_here, kept), jnp.bfloat16),
            pltpu.VMEM((inputs_here * group, 128), jnp.float32),
        ],
        compiler_params=pltpu.CompilerParams(vmem_limit_bytes=VMEM_LIMIT),
        cost_estimate=pl.CostEstimate(
            flops=8 * inputs_here * sample_count,
            bytes_accessed=4 * inputs_here * sample_count,
            transcendentals=0,
        ),
    )(history, filter_taps, voltages)


def on_device_steps(voltages, filter_taps, delays, channel_flags):
    inputs_here = voltages.shape[0]
    fft_length = filter_taps.shape[1]
    feeds, times = lax.axis_size("feed"), lax.axis_size("tm")
    filtered = filter_frames(voltages, filter_taps)
    frame_total = filtered.shape[1] * times
    owned = channel_flags.shape[0]
    kept = owned // times
    chunks = 4 if kept % 4 == 0 else 1
    width = kept // chunks
    block = 16 if inputs_here % 16 == 0 else inputs_here

    local_flags = lax.dynamic_slice_in_dim(
        channel_flags, lax.axis_index("tm") * kept, kept, 0
    ).astype(jnp.float32)
    flag_parts = (local_flags * (1.0 / (SEND_PEAK * frame_total))).reshape(chunks, width)
    scale = 1.0 / math.sqrt(fft_length)
    order = np.arange(feeds * owned).reshape(feeds, times, chunks, width)
    place = lax.axis_index("tm")

    def summed(vis, flags):
        total = 0.0
        for shift in range(times):
            target = lax.rem(place + shift, times)
            part = lax.dynamic_index_in_dim(vis, target, 0, keepdims=False)
            if shift:
                route = [(i, (i + shift) % times) for i in range(times)]
                part = lax.ppermute(part, "tm", route)
            part = part.astype(jnp.float32)
            count = part.shape[2]
            total = total + part[:, :count] * jnp.exp2(part[:, count:, :1][:, :1])
        return total * flags[:, None, None]

    results = []
    sent = []
    for k in range(chunks):
        channels = order[:, :, k].reshape(-1)
        table = jnp.asarray(table_rows(channels, fft_length))
        angles = 2.0 * math.pi / fft_length * jnp.asarray(channels, jnp.float32)[None, :, None]
        angles = angles * delays.reshape(-1, 1, block)
        if k >= 2:
            filtered, sent[k - 2] = lax.optimization_barrier((filtered, sent[k - 2]))
            results.append(summed(sent[k - 2], flag_parts[k - 2]))
        spectra = dft_call(table, jnp.cos(angles) * scale, jnp.sin(angles) * scale, filtered)
        spectra = spectra.reshape(feeds, times * width, inputs_here, spectra.shape[2])
        if k >= 3:
            spectra, results[k - 3] = lax.optimization_barrier((spectra, results[k - 3]))
        turned = lax.all_to_all(spectra, "feed", split_axis=0, concat_axis=0, tiled=True)
        if k >= 2:
            turned, results[k - 2] = lax.optimization_barrier((turned, results[k - 2]))
        vis = gram_call(turned).astype(jnp.float16)
        sent.append(vis.reshape(times, width, vis.shape[1], vis.shape[2]))
    for k in range(len(results), chunks):
        results.append(summed(sent[k], flag_parts[k]))
    return jnp.concatenate(results, axis=0)


VMEM_WHOLE = 63 * 1000 * 1000
MESH = pl.DeviceIdType.MESH
HALF = 16
GROUP = 16
UNITS = 4
LEVELS = 32760.0
NOTE_ROWS = 16
RING = 4
DIRECT = 2


def whole_kernel(
    volt_ref, taps_ref, table_ref, cos_ref, sin_ref, out_ref,
    stage, history, filtered, turned, send, recv, own, far, zsend, zrecv, relay,
    stage_sem, history_sems, send_sem, recv_sem, self_sem, zsend_sem, zrecv_sem, relay_sem, out_sem,
):
    feeds, times = lax.axis_size("feed"), lax.axis_size("tm")
    me, place = lax.axis_index("feed"), lax.axis_index("tm")
    inputs, sample_count = volt_ref.shape
    tap_count, fft_length = taps_ref.shape
    frames = sample_count // fft_length
    kept = tap_count - 1
    halves = inputs // HALF
    chunks = table_ref.shape[0]
    rows = table_ref.shape[1] // 2
    unit_count = chunks * UNITS
    relayed = relay.shape[0]
    total = feeds * inputs
    width = 128
    parts = frames // width
    part_groups = width // GROUP

    barrier = pltpu.get_barrier_semaphore()
    for s in range(1, feeds):
        pl.semaphore_signal(barrier, inc=1, device_id=(me ^ s, place), device_id_type=MESH)
    for s in range(1, times):
        other = lax.rem(place + s, times)
        pl.semaphore_signal(barrier, inc=1, device_id=(me, other), device_id_type=MESH)
    pl.semaphore_wait(barrier, feeds + times - 2)

    def history_copy():
        return pltpu.make_async_remote_copy(
            src_ref=volt_ref.at[:, pl.ds(sample_count - kept * fft_length, kept * fft_length)],
            dst_ref=history,
            send_sem=history_sems.at[0],
            recv_sem=history_sems.at[1],
            device_id=(me, place + 1),
            device_id_type=MESH,
        )

    @pl.when(place < times - 1)
    def _():
        history_copy().start()

    def block_copies(h, part, step):
        g = part * part_groups + lax.rem(step + 1, part_groups)
        slot = lax.rem(step, 2)
        at = pl.ds(pl.multiple_of(h * HALF, HALF), HALF)
        first = pl.multiple_of(jnp.maximum(g * GROUP - kept, 0) * fft_length, 128)
        later = pltpu.make_async_copy(
            volt_ref.at[at, pl.ds(first, (GROUP + kept) * fft_length)],
            stage.at[slot],
            stage_sem.at[slot],
        )
        start = pltpu.make_async_copy(
            volt_ref.at[at, pl.ds(0, GROUP * fft_length)],
            stage.at[slot, :, pl.ds(kept * fft_length, GROUP * fft_length)],
            stage_sem.at[slot],
        )
        return g, slot, later, start

    def block_start(h, part, step):
        g, _, later, start = block_copies(h, part, step)

        @pl.when(g > 0)
        def _():
            later.start()

        @pl.when(g == 0)
        def _():
            start.start()

    def filter_part(h, part):
        block_start(h, part, 0)

        def step_body(step, unused):
            @pl.when(step + 1 < part_groups)
            def _():
                block_start(h, part, step + 1)

            g, slot, later, start = block_copies(h, part, step)

            @pl.when(g > 0)
            def _():
                later.wait()

            @pl.when(g == 0)
            def _():
                start.wait()

                @pl.when(place == 0)
                def _():
                    stage[slot, :, : kept * fft_length] = jnp.zeros(
                        (HALF, kept * fft_length), jnp.bfloat16
                    )

                @pl.when(place > 0)
                def _():
                    @pl.when(h == 0)
                    def _():
                        history_copy().wait_recv()

                    at = pl.ds(pl.multiple_of(h * HALF, HALF), HALF)
                    stage[slot, :, : kept * fft_length] = history[at, :]

            def piece(p, unused):
                lanes = pl.multiple_of(p * 128, 128)
                taps = [taps_ref[t : t + 1, pl.ds(lanes, 128)] for t in range(tap_count)]

                def frame(j):
                    column = pl.multiple_of(j * fft_length + lanes, 128)
                    return stage[slot, :, pl.ds(column, 128)].astype(jnp.float32)

                window = [frame(j) for j in range(kept)]
                for m in range(GROUP):
                    window.append(frame(m + kept))
                    value = taps[0] * window[-1]
                    for t in range(1, tap_count):
                        value = value + taps[t] * window[-1 - t]
                    turned[0, pl.ds(m, HALF, stride=GROUP), :] = value
                result = turned[0, : HALF * GROUP].reshape(HALF, GROUP, 128).astype(jnp.bfloat16)
                at = pl.ds(pl.multiple_of(h * HALF, HALF), HALF)
                of = pl.ds(pl.multiple_of(g * GROUP, GROUP), GROUP)
                filtered[at, of, pl.ds(lanes, 128)] = result
                return unused

            return lax.fori_loop(0, fft_length // 128, piece, unused)

        lax.fori_loop(0, part_groups, step_body, 0)

    def transform(k, h, first, count):
        slot = lax.rem(k, 2)
        cosine_all = jnp.transpose(cos_ref[k, h])
        sine_all = jnp.transpose(sin_ref[k, h])
        span = pl.ds(pl.multiple_of(first * width, width), count * width)
        for i in range(HALF):
            raw = lax.dot_general(
                table_ref[k], filtered[h * HALF + i, span], (((1,), (1,)), ((), ())),
                preferred_element_type=jnp.float32,
            )
            real, imag = raw[:rows], raw[rows:]
            cosine = cosine_all[:, i : i + 1]
            sine = sine_all[:, i : i + 1]
            both = (real * cosine + imag * sine, imag * cosine - real * sine)
            for part in range(count):
                for q in range(2):
                    turned[2 * part + q, pl.ds(i, rows, stride=HALF), :] = both[q][
                        :, part * width : (part + 1) * width
                    ]
        for j in range(2 * count):
            value = turned[j].reshape(UNITS, feeds, times, HALF, width).astype(jnp.bfloat16)
            lanes = pl.ds(pl.multiple_of((2 * first + j) * width, width), width)
            send[slot, :, :, :, half_rows(h), lanes] = value

    def half_rows(h):
        return pl.ds(pl.multiple_of(h * HALF, HALF), HALF)

    def head_copies(at, lanes):
        copies = []
        for s in range(1, feeds):
            peer = me ^ s
            copies.append(
                pltpu.make_async_remote_copy(
                    src_ref=send.at[0, :, peer, :, at, lanes],
                    dst_ref=recv.at[pl.ds(0, UNITS), me, :, at, lanes],
                    send_sem=send_sem.at[0, s],
                    recv_sem=recv_sem.at[0, s],
                    device_id=(peer, place),
                    device_id_type=MESH,
                )
            )
        mine = pltpu.make_async_copy(
            send.at[0, :, me, :, at, lanes],
            recv.at[pl.ds(0, UNITS), me, :, at, lanes],
            self_sem.at[0],
        )
        return copies, mine

    def unit_copies(k, u):
        slot = lax.rem(k, 2)
        g = k * UNITS + u
        copies = []
        for s in range(1, feeds):
            peer = me ^ s
            copies.append(
                pltpu.make_async_remote_copy(
                    src_ref=send.at[slot, u, peer],
                    dst_ref=recv.at[g, me],
                    send_sem=send_sem.at[g, s],
                    recv_sem=recv_sem.at[g, s],
                    device_id=(peer, place),
                    device_id_type=MESH,
                )
            )
        mine = pltpu.make_async_copy(send.at[slot, u, me], recv.at[g, me], self_sem.at[g])
        return copies, mine

    all_rows, all_lanes = pl.ds(0, inputs), pl.ds(0, 2 * frames)

    def send_units(k):
        def one(u, unused):
            copies, mine = unit_copies(k, u)
            for copy in copies:
                copy.start()
            mine.start()
            return unused

        lax.fori_loop(0, UNITS, one, 0)

    def sent(k):
        @pl.when(k == 0)
        def _():
            copies, _ = head_copies(all_rows, all_lanes)
            for copy in copies:
                copy.wait_send()

        @pl.when(k > 0)
        def _():
            def one(u, unused):
                copies, _ = unit_copies(k, u)
                for copy in copies:
                    copy.wait_send()
                return unused

            lax.fori_loop(0, UNITS, one, 0)

    def arrived(g):
        @pl.when(g == 0)
        def _():
            copies, mine = head_copies(all_rows, all_lanes)
            for copy in copies:
                copy.wait_recv()
            mine.wait()

        @pl.when(g >= UNITS)
        def _():
            copies, mine = unit_copies(g // UNITS, lax.rem(g, UNITS))
            for copy in copies:
                copy.wait_recv()
            mine.wait()

    row = lax.broadcasted_iota(jnp.int32, (total, total), 0)
    column = lax.broadcasted_iota(jnp.int32, (total, total), 1)
    dims = (((1,), (1,)), ((), ()))

    middle = jnp.logical_and(place > 0, place < times - 1)

    def zcopy(g, s):
        return pltpu.make_async_remote_copy(
            src_ref=zsend.at[lax.rem(g, RING), s - 1],
            dst_ref=zrecv.at[g, s - 1],
            send_sem=zsend_sem.at[g, s],
            recv_sem=zrecv_sem.at[g, s],
            device_id=(me, place ^ s),
            device_id_type=MESH,
        )

    def relay_copy(g):
        return pltpu.make_async_remote_copy(
            src_ref=zsend.at[lax.rem(g, RING), 2],
            dst_ref=relay.at[g],
            send_sem=zsend_sem.at[g, 3],
            recv_sem=relay_sem.at[g],
            device_id=(me, place ^ 1),
            device_id_type=MESH,
        )

    def out_copy(g):
        slot = lax.rem(g, RING)
        return pltpu.make_async_copy(own.at[slot], out_ref.at[g], out_sem.at[slot])

    def gram(g):
        arrived(g)
        slot = lax.rem(g, RING)

        @pl.when(g >= RING)
        def _():
            for s in range(1, times):
                zcopy(g - RING, s).wait_send()
            out_copy(g - RING).wait()

        for s in (1, 3, 2, 0):
            slab = recv[g, :, place ^ s].reshape(total, 2 * frames)
            columns = [slab[:, j * width : (j + 1) * width] for j in range(2 * parts)]
            swapped = [-columns[j - 1] if j % 2 else columns[j + 1] for j in range(2 * parts)]
            swapped = jnp.concatenate(swapped, axis=1)
            real = lax.dot_general(slab, slab, dims, preferred_element_type=jnp.float32)
            imag = lax.dot_general(swapped, slab, dims, preferred_element_type=jnp.float32)
            packed = jnp.where(row <= column, real, imag)
            if s == 0:
                own[slot] = packed
            elif s == 1:
                code(packed, slot, s)
                zcopy(g, s).start()
            elif s == 3:
                code(packed, slot, s)
                passed_on = jnp.logical_and(jnp.logical_not(middle), g < relayed)

                @pl.when(passed_on)
                def _():
                    relay_copy(g).start()

                @pl.when(jnp.logical_not(passed_on))
                def _():
                    zcopy(g, s).start()
            else:
                held_back = jnp.logical_and(middle, g < relayed)

                @pl.when(held_back)
                def _():
                    far[lax.rem(g, 2)] = packed

                @pl.when(jnp.logical_not(held_back))
                def _():
                    code(packed, slot, s)
                    zcopy(g, s).start()

    def code(packed, slot, s):
        diagonal = jnp.where(row == column, packed, 0.0)
        powers = [
            jnp.ceil(0.5 * jnp.log2(jnp.maximum(jnp.sum(diagonal, axis=a, keepdims=True), 1e-30)))
            for a in range(2)
        ]
        scaled = packed * (LEVELS * jnp.exp2(-powers[0])) * jnp.exp2(-powers[1])
        zsend[slot, s - 1, :total] = jnp.round(scaled).astype(jnp.int32).astype(jnp.int16)
        note = jnp.broadcast_to(powers[0], (NOTE_ROWS, total))
        zsend[slot, s - 1, total:] = note.astype(jnp.int32).astype(jnp.int16)

    def decoded(value, note):
        across = jnp.exp2(note.astype(jnp.int32).astype(jnp.float32))[:1]
        down = jnp.sum(jnp.where(row == column, across, 0.0), axis=1, keepdims=True)
        return value.astype(jnp.int32).astype(jnp.float32) * across * (down * (1.0 / LEVELS))

    def pass_on(g):
        @pl.when(jnp.logical_and(middle, g < relayed))
        def _():
            relay_copy(g).wait_recv()
            both = far[lax.rem(g, 2)] + decoded(relay[g, :total], relay[g, total:])
            code(both, lax.rem(g, RING), 2)
            zcopy(g, 2).start()

    def finish(g):
        slot = lax.rem(g, RING)
        for s in (1, 2):
            zcopy(g, s).wait_recv()
            own[slot] += decoded(zrecv[g, s - 1, :total], zrecv[g, s - 1, total:])

        @pl.when(jnp.logical_or(middle, g >= relayed))
        def _():
            zcopy(g, 3).wait_recv()
            own[slot] += decoded(zrecv[g, 2, :total], zrecv[g, 2, total:])

        out_copy(g).start()

    def head(j, unused):
        h, part = j // parts, parts - 1 - lax.rem(j, parts)
        filter_part(h, part)
        transform(0, h, part, 1)
        copies, mine = head_copies(
            half_rows(h), pl.ds(pl.multiple_of(part * 2 * width, 2 * width), 2 * width)
        )
        for copy in copies:
            copy.start()
        mine.start()
        return unused

    lax.fori_loop(0, halves * parts, head, 0)

    lag = RING - 1

    def units_of(k):
        def one(u, unused):
            g = k * UNITS + u
            gram(g)

            @pl.when(g >= 1)
            def _():
                pass_on(g - 1)

            @pl.when(g >= lag)
            def _():
                finish(g - lag)

            return unused

        lax.fori_loop(0, UNITS, one, 0)

    def main(k, unused):
        @pl.when(k < chunks)
        def _():
            @pl.when(k >= 2)
            def _():
                sent(k - 2)

            def half(h, unused):
                transform(k, h, 0, parts)
                return unused

            lax.fori_loop(0, halves, half, 0)
            send_units(k)

        units_of(k - 1)
        return unused

    lax.fori_loop(1, chunks + 1, main, 0)

    def last(j, unused):
        finish(unit_count - lag + j)
        return unused

    lax.fori_loop(0, lag, last, 0)

    for k in range(max(chunks - 2, 0), chunks):
        sent(k)

    def drain(j, unused):
        g = unit_count - RING + j
        for s in range(1, times):
            zcopy(g, s).wait_send()
        out_copy(g).wait()
        return unused

    lax.fori_loop(0, RING, drain, 0)

    @pl.when(place < times - 1)
    def _():
        history_copy().wait_send()


def whole_call(voltages, filter_taps, table, cosine, sine):
    feeds, times = lax.axis_size("feed"), lax.axis_size("tm")
    inputs, sample_count = voltages.shape
    tap_count, fft_length = filter_taps.shape
    frames = sample_count // fft_length
    chunks, rows = table.shape[0], table.shape[1] // 2
    units = chunks * UNITS
    total = feeds * inputs
    kept = tap_count - 1
    vmem = pl.BlockSpec(memory_space=pltpu.VMEM)
    return pl.pallas_call(
        whole_kernel,
        out_shape=jax.ShapeDtypeStruct((units, total, total), jnp.float32),
        in_specs=[pl.BlockSpec(memory_space=pl.ANY), vmem, vmem, vmem, vmem],
        out_specs=pl.BlockSpec(memory_space=pl.ANY),
        scratch_shapes=[
            pltpu.VMEM((2, HALF, (GROUP + kept) * fft_length), jnp.bfloat16),
            pltpu.VMEM((inputs, kept * fft_length), jnp.bfloat16),
            pltpu.VMEM((inputs, frames, fft_length), jnp.bfloat16),
            pltpu.VMEM((2 * frames // 128, rows * HALF, 128), jnp.float32),
            pltpu.VMEM((2, UNITS, feeds, times, inputs, 2 * frames), jnp.bfloat16),
            pltpu.VMEM((units, feeds, times, inputs, 2 * frames), jnp.bfloat16),
            pltpu.VMEM((RING, total, total), jnp.float32),
            pltpu.VMEM((2, total, total), jnp.float32),
            pltpu.VMEM((RING, times - 1, total + NOTE_ROWS, total), jnp.int16),
            pltpu.VMEM((units, times - 1, total + NOTE_ROWS, total), jnp.int16),
            pltpu.VMEM((units - DIRECT, total + NOTE_ROWS, total), jnp.int16),
            pltpu.SemaphoreType.DMA((2,)),
            pltpu.SemaphoreType.DMA((2,)),
            pltpu.SemaphoreType.DMA((units, feeds)),
            pltpu.SemaphoreType.DMA((units, feeds)),
            pltpu.SemaphoreType.DMA((units,)),
            pltpu.SemaphoreType.DMA((units, times)),
            pltpu.SemaphoreType.DMA((units, times)),
            pltpu.SemaphoreType.DMA((units - DIRECT,)),
            pltpu.SemaphoreType.DMA((RING,)),
        ],
        compiler_params=pltpu.CompilerParams(
            vmem_limit_bytes=VMEM_WHOLE, collective_id=0, has_side_effects=True
        ),
        cost_estimate=pl.CostEstimate(
            flops=8 * inputs * sample_count * 512,
            bytes_accessed=4 * inputs * sample_count,
            transcendentals=0,
        ),
    )(voltages, filter_taps, table, cosine, sine)


def whole_fits(voltages, filter_taps, channel_flags, feeds, times):
    inputs, frames = voltages.shape[0], voltages.shape[1] // filter_taps.shape[1]
    kept = channel_flags.shape[0] // times
    rows = UNITS * feeds * times
    if times != 4 or inputs % HALF or feeds & (feeds - 1) or kept % UNITS or frames % 128:
        return False
    if kept < 2 * UNITS or frames < 2 * GROUP:
        return False
    spectra = 2 * inputs * 2 * frames
    total = feeds * inputs
    held = 2 * inputs * voltages.shape[1]
    held += spectra * (2 * rows + kept * feeds * times) + 8 * frames * rows * HALF
    held += 2 * ((RING + kept) * (times - 1) + kept - DIRECT) * (total + NOTE_ROWS) * total
    held += 4 * (RING + 2) * total * total
    return held < VMEM_WHOLE - 3 * 1000 * 1000


def on_device_whole(voltages, filter_taps, delays, channel_flags):
    inputs = voltages.shape[0]
    fft_length = filter_taps.shape[1]
    feeds, times = lax.axis_size("feed"), lax.axis_size("tm")
    frame_total = voltages.shape[1] // fft_length * times
    owned = channel_flags.shape[0]
    kept = owned // times
    chunks = kept // UNITS
    order = np.arange(feeds * owned).reshape(feeds, times, chunks, UNITS)
    order = order.transpose(2, 3, 0, 1).reshape(chunks, -1)
    table = jnp.asarray(np.stack([table_rows(order[k], fft_length) for k in range(chunks)]))
    angles = 2.0 * math.pi / fft_length * jnp.asarray(order, jnp.float32)[:, None, :]
    angles = angles * delays[None, :, None]
    scale = 1.0 / math.sqrt(fft_length)
    shape = (chunks, inputs // HALF, HALF, order.shape[1])
    cosine = (jnp.cos(angles) * scale).reshape(shape)
    sine = (jnp.sin(angles) * scale).reshape(shape)
    vis = whole_call(voltages, filter_taps, table, cosine, sine)
    flags = lax.dynamic_slice_in_dim(channel_flags, lax.axis_index("tm") * kept, kept, 0)
    return vis * (flags.astype(jnp.float32) * (1.0 / frame_total))[:, None, None]


def on_device(voltages, filter_taps, delays, channel_flags):
    feeds, times = lax.axis_size("feed"), lax.axis_size("tm")
    if whole_fits(voltages, filter_taps, channel_flags, feeds, times):
        return on_device_whole(voltages, filter_taps, delays, channel_flags)
    return on_device_steps(voltages, filter_taps, delays, channel_flags)


def solution(mesh):
    in_specs = (P("feed", "tm"), P(), P("feed"), P("feed"))
    out_specs = P(("feed", "tm"), None, None)
    return jax.shard_map(
        on_device, mesh=mesh, in_specs=in_specs, out_specs=out_specs, check_vma=False
    )
```

```python
import functools
import math

import jax
import jax.numpy as jnp
import numpy as np
from jax import lax
from jax.experimental import pallas as pl
from jax.experimental.pallas import tpu as pltpu
from jax.sharding import PartitionSpec as P

VMEM_LIMIT = 56 * 1024 * 1024
SEND_PEAK = 16384.0
EXTRA_ROWS = 8


def passed_along(block, axis, distance):
    devices = range(lax.axis_size(axis))
    route = [(i - distance, i) for i in devices if i - distance in devices]
    return lax.ppermute(block, axis, route)


def table_rows(channels, fft_length):
    samples = np.arange(fft_length, dtype=np.int64)
    product = channels[:, None].astype(np.int64) * samples[None, :] % fft_length
    angles = product.astype(np.float32) * np.float32(2.0 * math.pi / fft_length)
    rows = np.concatenate([np.cos(angles), -np.sin(angles)], axis=0)
    return rows.astype(jnp.bfloat16)


def dft_kernel(table_ref, cos_ref, sin_ref, filtered_ref, out_ref, *turned):
    inputs, frames = filtered_ref.shape[0], filtered_ref.shape[1]
    rows = table_ref.shape[0] // 2
    width = 128
    for i in range(inputs):
        raw = lax.dot_general(
            table_ref[...], filtered_ref[i], (((1,), (1,)), ((), ())),
            preferred_element_type=jnp.float32,
        )
        real, imag = raw[:rows], raw[rows:]
        cosine = cos_ref[0, :, i : i + 1]
        sine = sin_ref[0, :, i : i + 1]
        both = (real * cosine + imag * sine, imag * cosine - real * sine)
        for q in range(2):
            for piece in range(frames // width):
                turned[q * (frames // width) + piece][pl.ds(i, rows, stride=inputs), :] = both[q][
                    :, piece * width : (piece + 1) * width
                ]
    for piece, ref in enumerate(turned):
        value = ref[...].reshape(rows, inputs, width).astype(jnp.bfloat16)
        out_ref[:, :, piece * width : (piece + 1) * width] = value


def dft_call(table, cosine, sine, filtered):
    blocks, rows, inputs = cosine.shape
    inputs_here, frames, fft_length = filtered.shape
    out_shape = jax.ShapeDtypeStruct((rows, inputs_here, 2 * frames), jnp.bfloat16)
    return pl.pallas_call(
        dft_kernel,
        out_shape=out_shape,
        grid=(blocks,),
        in_specs=[
            pl.BlockSpec((2 * rows, fft_length), lambda b: (0, 0)),
            pl.BlockSpec((1, rows, inputs), lambda b: (b, 0, 0)),
            pl.BlockSpec((1, rows, inputs), lambda b: (b, 0, 0)),
            pl.BlockSpec((inputs, frames, fft_length), lambda b: (b, 0, 0)),
        ],
        out_specs=pl.BlockSpec((rows, inputs, 2 * frames), lambda b: (0, b, 0)),
        scratch_shapes=[pltpu.VMEM((rows * inputs, 128), jnp.float32)] * (2 * frames // 128),
        compiler_params=pltpu.CompilerParams(vmem_limit_bytes=VMEM_LIMIT),
        cost_estimate=pl.CostEstimate(
            flops=10 * 4 * rows * inputs_here * frames * fft_length,
            bytes_accessed=2 * inputs_here * frames * (fft_length + 2 * rows),
            transcendentals=0,
        ),
    )(table, cosine, sine, filtered)


def gram_kernel(spectra_ref, vis_ref):
    sources, channels, inputs_here, columns = spectra_ref.shape
    total = sources * inputs_here
    half = columns // 2
    row = lax.broadcasted_iota(jnp.int32, (total, total), 0)
    column = lax.broadcasted_iota(jnp.int32, (total, total), 1)
    dims = (((1,), (1,)), ((), ()))
    for c in range(channels):
        slab = spectra_ref[:, c]
        if inputs_here % 16:
            slab = slab.astype(jnp.float32).reshape(total, columns).astype(jnp.bfloat16)
        else:
            slab = slab.reshape(total, columns)
        swapped = jnp.concatenate([slab[:, half:], -slab[:, :half]], axis=1)
        real = lax.dot_general(slab, slab, dims, preferred_element_type=jnp.float32)
        imag = lax.dot_general(swapped, slab, dims, preferred_element_type=jnp.float32)
        packed = jnp.where(row <= column, real, imag)
        peak = jnp.max(jnp.where(row == column, real, 0.0), axis=(0, 1), keepdims=True)
        peak = jnp.maximum(peak, 1e-30)
        power = jnp.ceil(jnp.log2(peak))
        vis_ref[c, :total] = packed * (SEND_PEAK * jnp.exp2(-power))
        vis_ref[c, total:] = jnp.broadcast_to(power, (EXTRA_ROWS, total))


def gram_call(spectra):
    sources, channels, inputs_here, columns = spectra.shape
    total = sources * inputs_here
    step = 2 if channels % 2 == 0 else 1
    return pl.pallas_call(
        gram_kernel,
        out_shape=jax.ShapeDtypeStruct((channels, total + EXTRA_ROWS, total), jnp.float32),
        grid=(channels // step,),
        in_specs=[pl.BlockSpec((sources, step, inputs_here, columns), lambda b: (0, b, 0, 0))],
        out_specs=pl.BlockSpec((step, total + EXTRA_ROWS, total), lambda b: (b, 0, 0)),
        compiler_params=pltpu.CompilerParams(vmem_limit_bytes=VMEM_LIMIT),
        cost_estimate=pl.CostEstimate(
            flops=40 * 4 * channels * total * total * columns,
            bytes_accessed=2 * channels * total * (columns + 2 * total),
            transcendentals=0,
        ),
    )(spectra)


def filter_kernel(history_ref, taps_ref, block_ref, out_ref, carry, turned):
    tap_count, fft_length = taps_ref.shape
    inputs, group = out_ref.shape[0], out_ref.shape[1]
    kept = tap_count - 1

    @pl.when(pl.program_id(0) == 0)
    def _():
        carry[...] = history_ref[...]

    def piece(p, unused):
        lanes = pl.multiple_of(p * 128, 128)
        taps = [taps_ref[t : t + 1, pl.ds(lanes, 128)] for t in range(tap_count)]
        frames = [
            carry[:, pl.ds(pl.multiple_of(h * fft_length + lanes, 128), 128)].astype(jnp.float32)
            for h in range(kept)
        ]
        for m in range(group):
            start = pl.multiple_of(m * fft_length + lanes, 128)
            frames.append(block_ref[:, pl.ds(start, 128)].astype(jnp.float32))
            value = taps[0] * frames[-1]
            for t in range(1, tap_count):
                value = value + taps[t] * frames[-1 - t]
            turned[pl.ds(m, inputs, stride=group), :] = value
        result = turned[...].reshape(inputs, group, 128).astype(jnp.bfloat16)
        out_ref[:, :, pl.ds(lanes, 128)] = result
        return unused

    lax.fori_loop(0, fft_length // 128, piece, 0)
    carry[...] = block_ref[:, (group - kept) * fft_length :]


def filter_frames(voltages, filter_taps):
    inputs_here, sample_count = voltages.shape
    tap_count, fft_length = filter_taps.shape
    frames = sample_count // fft_length
    kept = (tap_count - 1) * fft_length
    group = 16
    history = passed_along(voltages[:, sample_count - kept :], "tm", 1)
    return pl.pallas_call(
        filter_kernel,
        out_shape=jax.ShapeDtypeStruct((inputs_here, frames, fft_length), jnp.bfloat16),
        grid=(frames // group,),
        in_specs=[
            pl.BlockSpec((inputs_here, kept), lambda b: (0, 0)),
            pl.BlockSpec((tap_count, fft_length), lambda b: (0, 0)),
            pl.BlockSpec((inputs_here, group * fft_length), lambda b: (0, b)),
        ],
        out_specs=pl.BlockSpec((inputs_here, group, fft_length), lambda b: (0, b, 0)),
        scratch_shapes=[
            pltpu.VMEM((inputs_here, kept), jnp.bfloat16),
            pltpu.VMEM((inputs_here * group, 128), jnp.float32),
        ],
        compiler_params=pltpu.CompilerParams(vmem_limit_bytes=VMEM_LIMIT),
        cost_estimate=pl.CostEstimate(
            flops=8 * inputs_here * sample_count,
            bytes_accessed=4 * inputs_here * sample_count,
            transcendentals=0,
        ),
    )(history, filter_taps, voltages)


def on_device_steps(voltages, filter_taps, delays, channel_flags):
    inputs_here = voltages.shape[0]
    fft_length = filter_taps.shape[1]
    feeds, times = lax.axis_size("feed"), lax.axis_size("tm")
    filtered = filter_frames(voltages, filter_taps)
    frame_total = filtered.shape[1] * times
    owned = channel_flags.shape[0]
    kept = owned // times
    chunks = 4 if kept % 4 == 0 else 1
    width = kept // chunks
    block = 16 if inputs_here % 16 == 0 else inputs_here

    local_flags = lax.dynamic_slice_in_dim(
        channel_flags, lax.axis_index("tm") * kept, kept, 0
    ).astype(jnp.float32)
    flag_parts = (local_flags * (1.0 / (SEND_PEAK * frame_total))).reshape(chunks, width)
    scale = 1.0 / math.sqrt(fft_length)
    order = np.arange(feeds * owned).reshape(feeds, times, chunks, width)
    place = lax.axis_index("tm")

    def summed(vis, flags):
        total = 0.0
        for shift in range(times):
            target = lax.rem(place + shift, times)
            part = lax.dynamic_index_in_dim(vis, target, 0, keepdims=False)
            if shift:
                route = [(i, (i + shift) % times) for i in range(times)]
                part = lax.ppermute(part, "tm", route)
            part = part.astype(jnp.float32)
            count = part.shape[2]
            total = total + part[:, :count] * jnp.exp2(part[:, count:, :1][:, :1])
        return total * flags[:, None, None]

    results = []
    sent = []
    for k in range(chunks):
        channels = order[:, :, k].reshape(-1)
        table = jnp.asarray(table_rows(channels, fft_length))
        angles = 2.0 * math.pi / fft_length * jnp.asarray(channels, jnp.float32)[None, :, None]
        angles = angles * delays.reshape(-1, 1, block)
        if k >= 2:
            filtered, sent[k - 2] = lax.optimization_barrier((filtered, sent[k - 2]))
            results.append(summed(sent[k - 2], flag_parts[k - 2]))
        spectra = dft_call(table, jnp.cos(angles) * scale, jnp.sin(angles) * scale, filtered)
        spectra = spectra.reshape(feeds, times * width, inputs_here, spectra.shape[2])
        if k >= 3:
            spectra, results[k - 3] = lax.optimization_barrier((spectra, results[k - 3]))
        turned = lax.all_to_all(spectra, "feed", split_axis=0, concat_axis=0, tiled=True)
        if k >= 2:
            turned, results[k - 2] = lax.optimization_barrier((turned, results[k - 2]))
        vis = gram_call(turned).astype(jnp.float16)
        sent.append(vis.reshape(times, width, vis.shape[1], vis.shape[2]))
    for k in range(len(results), chunks):
        results.append(summed(sent[k], flag_parts[k]))
    return jnp.concatenate(results, axis=0)


VMEM_WHOLE = 64 * 1000 * 1000
MESH = pl.DeviceIdType.MESH
HALF = 16
GROUP = 16
UNITS = 4
LEVELS = 32760.0
NOTE_ROWS = 16
RING = 4
DIRECT = 1
STAGES = 4
PITCH = GROUP + 1


def whole_kernel(
    volt_ref, taps_ref, table_ref, cos_ref, sin_ref, out_ref,
    stage, history, filtered, turned, send, recv, own, far, zsend, zrecv, relay,
    stage_sem, history_sems, send_sem, recv_sem, self_sem, zsend_sem, zrecv_sem, relay_sem, out_sem,
):
    feeds, times = lax.axis_size("feed"), lax.axis_size("tm")
    me, place = lax.axis_index("feed"), lax.axis_index("tm")
    inputs, sample_count = volt_ref.shape
    tap_count, fft_length = taps_ref.shape
    frames = sample_count // fft_length
    kept = tap_count - 1
    halves = inputs // HALF
    chunks = table_ref.shape[0]
    rows = table_ref.shape[1] // 2
    unit_count = chunks * UNITS
    relayed = relay.shape[0]
    total = feeds * inputs
    width = 128
    parts = frames // width
    part_groups = width // GROUP

    barrier = pltpu.get_barrier_semaphore()
    for s in range(1, feeds):
        pl.semaphore_signal(barrier, inc=1, device_id=(me ^ s, place), device_id_type=MESH)
    for s in range(1, times):
        other = lax.rem(place + s, times)
        pl.semaphore_signal(barrier, inc=1, device_id=(me, other), device_id_type=MESH)
    def history_copy():
        return pltpu.make_async_remote_copy(
            src_ref=volt_ref.at[:, pl.ds(sample_count - kept * fft_length, kept * fft_length)],
            dst_ref=history,
            send_sem=history_sems.at[0],
            recv_sem=history_sems.at[1],
            device_id=(me, place + 1),
            device_id_type=MESH,
        )

    head_steps = halves * parts * part_groups

    def quarter(j):
        return j // parts, parts - 1 - lax.rem(j, parts)

    def block_copies(n):
        h, part = quarter(n // part_groups)
        g = part * part_groups + lax.rem(lax.rem(n, part_groups) + 1, part_groups)
        slot = lax.rem(n, STAGES)
        at = half_rows(h)
        first = pl.multiple_of(jnp.maximum(g * GROUP - kept, 0) * fft_length, 128)
        later = pltpu.make_async_copy(
            volt_ref.at[at, pl.ds(first, (GROUP + kept) * fft_length)],
            stage.at[slot],
            stage_sem.at[slot],
        )
        start = pltpu.make_async_copy(
            volt_ref.at[at, pl.ds(0, GROUP * fft_length)],
            stage.at[slot, :, pl.ds(kept * fft_length, GROUP * fft_length)],
            stage_sem.at[slot],
        )
        return g, slot, later, start

    def block_start(n):
        g, _, later, start = block_copies(n)

        @pl.when(g > 0)
        def _():
            later.start()

        @pl.when(g == 0)
        def _():
            start.start()

    def filter_part(j):
        h, _ = quarter(j)

        def step_body(step, unused):
            n = j * part_groups + step

            @pl.when(n + STAGES - 1 < head_steps)
            def _():
                block_start(n + STAGES - 1)

            g, slot, later, start = block_copies(n)

            @pl.when(g > 0)
            def _():
                later.wait()

            @pl.when(g == 0)
            def _():
                start.wait()

                @pl.when(place == 0)
                def _():
                    stage[slot, :, : kept * fft_length] = jnp.zeros(
                        (HALF, kept * fft_length), jnp.bfloat16
                    )

                @pl.when(place > 0)
                def _():
                    @pl.when(h == 0)
                    def _():
                        history_copy().wait_recv()

                    stage[slot, :, : kept * fft_length] = history[half_rows(h), :]

            of = pl.ds(pl.multiple_of(g * GROUP, GROUP), GROUP)
            for lane in range(0, fft_length, width):
                taps = [taps_ref[t : t + 1, lane : lane + width] for t in range(tap_count)]

                def frame(j):
                    column = j * fft_length + lane
                    return stage[slot, :, column : column + width].astype(jnp.float32)

                window = [frame(j) for j in range(kept)]
                for m in range(GROUP):
                    window.append(frame(m + kept))
                    value = taps[0] * window[-1]
                    for t in range(1, tap_count):
                        value = value + taps[t] * window[-1 - t]
                    turned[0, pl.ds(m, HALF, stride=PITCH), :] = value
                for i in range(HALF):
                    rows_here = turned[0, i * PITCH : i * PITCH + GROUP]
                    filtered[h * HALF + i, of, lane : lane + width] = rows_here.astype(jnp.bfloat16)
            return unused

        lax.fori_loop(0, part_groups, step_body, 0)

    def transform(k, h, part):
        slot = lax.rem(k, 2)
        span = pl.ds(pl.multiple_of(part * width, width), width)
        block = filtered[half_rows(h), span].reshape(HALF * width, fft_length)
        raw = lax.dot_general(
            block, table_ref[k], (((1,), (1,)), ((), ())), preferred_element_type=jnp.float32
        )
        for i in range(HALF):
            here = raw[i * width : (i + 1) * width]
            real, imag = here[:, :rows], here[:, rows:]
            cosine = cos_ref[k, h, i : i + 1]
            sine = sin_ref[k, h, i : i + 1]
            both = (real * cosine + imag * sine, imag * cosine - real * sine)
            for q in range(2):
                turned[q, pl.ds(i, rows, stride=PITCH), :] = jnp.transpose(both[q])
        for q in range(2):
            lanes = pl.ds(pl.multiple_of((2 * part + q) * width, width), width)
            for r in range(rows):
                u, f, t = r // (feeds * times), r // times % feeds, r % times
                value = turned[q, r * PITCH : r * PITCH + HALF].astype(jnp.bfloat16)
                send[slot, u, f, t, half_rows(h), lanes] = value

    def half_rows(h):
        return pl.ds(pl.multiple_of(h * HALF, HALF), HALF)

    def head_copies(at, lanes):
        copies = []
        for s in range(1, feeds):
            peer = me ^ s
            copies.append(
                pltpu.make_async_remote_copy(
                    src_ref=send.at[0, :, peer, :, at, lanes],
                    dst_ref=recv.at[pl.ds(0, UNITS), me, :, at, lanes],
                    send_sem=send_sem.at[0, s],
                    recv_sem=recv_sem.at[0, s],
                    device_id=(peer, place),
                    device_id_type=MESH,
                )
            )
        mine = pltpu.make_async_copy(
            send.at[0, :, me, :, at, lanes],
            recv.at[pl.ds(0, UNITS), me, :, at, lanes],
            self_sem.at[0],
        )
        return copies, mine

    def unit_copies(k, u):
        slot = lax.rem(k, 2)
        g = k * UNITS + u
        copies = []
        for s in range(1, feeds):
            peer = me ^ s
            copies.append(
                pltpu.make_async_remote_copy(
                    src_ref=send.at[slot, u, peer],
                    dst_ref=recv.at[g, me],
                    send_sem=send_sem.at[g, s],
                    recv_sem=recv_sem.at[g, s],
                    device_id=(peer, place),
                    device_id_type=MESH,
                )
            )
        mine = pltpu.make_async_copy(send.at[slot, u, me], recv.at[g, me], self_sem.at[g])
        return copies, mine

    all_rows, all_lanes = pl.ds(0, inputs), pl.ds(0, 2 * frames)

    def send_units(k):
        def one(u, unused):
            copies, mine = unit_copies(k, u)
            for copy in copies:
                copy.start()
            mine.start()
            return unused

        lax.fori_loop(0, UNITS, one, 0)

    def sent(k):
        @pl.when(k == 0)
        def _():
            copies, _ = head_copies(all_rows, all_lanes)
            for copy in copies:
                copy.wait_send()

        @pl.when(k > 0)
        def _():
            def one(u, unused):
                copies, _ = unit_copies(k, u)
                for copy in copies:
                    copy.wait_send()
                return unused

            lax.fori_loop(0, UNITS, one, 0)

    def arrived(g):
        @pl.when(g == 0)
        def _():
            copies, mine = head_copies(all_rows, all_lanes)
            for copy in copies:
                copy.wait_recv()
            mine.wait()

        @pl.when(g >= UNITS)
        def _():
            copies, mine = unit_copies(g // UNITS, lax.rem(g, UNITS))
            for copy in copies:
                copy.wait_recv()
            mine.wait()

    row = lax.broadcasted_iota(jnp.int32, (total, total), 0)
    column = lax.broadcasted_iota(jnp.int32, (total, total), 1)
    dims = (((1,), (1,)), ((), ()))

    middle = jnp.logical_and(place > 0, place < times - 1)

    def zcopy(g, s):
        return pltpu.make_async_remote_copy(
            src_ref=zsend.at[lax.rem(g, RING), s - 1],
            dst_ref=zrecv.at[g, s - 1],
            send_sem=zsend_sem.at[g, s],
            recv_sem=zrecv_sem.at[g, s],
            device_id=(me, place ^ s),
            device_id_type=MESH,
        )

    def relay_copy(g):
        return pltpu.make_async_remote_copy(
            src_ref=zsend.at[lax.rem(g, RING), 2],
            dst_ref=relay.at[g],
            send_sem=zsend_sem.at[g, 3],
            recv_sem=relay_sem.at[g],
            device_id=(me, place ^ 1),
            device_id_type=MESH,
        )

    def out_copy(g):
        slot = lax.rem(g, RING)
        return pltpu.make_async_copy(own.at[slot], out_ref.at[g], out_sem.at[slot])

    def gram(g):
        arrived(g)
        slot = lax.rem(g, RING)

        @pl.when(g >= RING)
        def _():
            for s in range(1, times):
                zcopy(g - RING, s).wait_send()
            out_copy(g - RING).wait()

        for s in (1, 3, 2, 0):
            slab = recv[g, :, place ^ s].reshape(total, 2 * frames)
            columns = [slab[:, j * width : (j + 1) * width] for j in range(2 * parts)]
            swapped = [-columns[j - 1] if j % 2 else columns[j + 1] for j in range(2 * parts)]
            swapped = jnp.concatenate(swapped, axis=1)
            real = lax.dot_general(slab, slab, dims, preferred_element_type=jnp.float32)
            imag = lax.dot_general(swapped, slab, dims, preferred_element_type=jnp.float32)
            packed = jnp.where(row <= column, real, imag)
            if s == 0:
                own[slot] = packed
            elif s == 1:
                code(packed, slot, s)
                zcopy(g, s).start()
            elif s == 3:
                code(packed, slot, s)
                passed_on = jnp.logical_and(jnp.logical_not(middle), g < relayed)

                @pl.when(passed_on)
                def _():
                    relay_copy(g).start()

                @pl.when(jnp.logical_not(passed_on))
                def _():
                    zcopy(g, s).start()
            else:
                held_back = jnp.logical_and(middle, g < relayed)

                @pl.when(held_back)
                def _():
                    far[lax.rem(g, 2)] = packed

                @pl.when(jnp.logical_not(held_back))
                def _():
                    code(packed, slot, s)
                    zcopy(g, s).start()

    def code(packed, slot, s):
        diagonal = jnp.where(row == column, packed, 0.0)
        powers = [
            jnp.ceil(0.5 * jnp.log2(jnp.maximum(jnp.sum(diagonal, axis=a, keepdims=True), 1e-30)))
            for a in range(2)
        ]
        scaled = packed * (LEVELS * jnp.exp2(-powers[0])) * jnp.exp2(-powers[1])
        zsend[slot, s - 1, :total] = jnp.round(scaled).astype(jnp.int32).astype(jnp.int16)
        note = jnp.broadcast_to(powers[0], (NOTE_ROWS, total))
        zsend[slot, s - 1, total:] = note.astype(jnp.int32).astype(jnp.int16)

    def decoded(value, note):
        across = jnp.exp2(note.astype(jnp.int32).astype(jnp.float32))[:1]
        down = jnp.sum(jnp.where(row == column, across, 0.0), axis=1, keepdims=True)
        return value.astype(jnp.int32).astype(jnp.float32) * across * (down * (1.0 / LEVELS))

    def pass_on(g):
        @pl.when(jnp.logical_and(middle, g < relayed))
        def _():
            relay_copy(g).wait_recv()
            both = far[lax.rem(g, 2)] + decoded(relay[g, :total], relay[g, total:])
            code(both, lax.rem(g, RING), 2)
            zcopy(g, 2).start()

    def finish(g):
        slot = lax.rem(g, RING)
        for s in (1, 2):
            zcopy(g, s).wait_recv()
            own[slot] += decoded(zrecv[g, s - 1, :total], zrecv[g, s - 1, total:])

        @pl.when(jnp.logical_or(middle, g >= relayed))
        def _():
            zcopy(g, 3).wait_recv()
            own[slot] += decoded(zrecv[g, 2, :total], zrecv[g, 2, total:])

        out_copy(g).start()

    for n in range(STAGES - 1):
        block_start(jnp.int32(n))

    def head(j, unused):
        h, part = quarter(j)
        filter_part(j)

        transform(0, h, part)

        @pl.when(j == 0)
        def _():
            pl.semaphore_wait(barrier, feeds + times - 2)

            @pl.when(place < times - 1)
            def _():
                history_copy().start()

        copies, mine = head_copies(
            half_rows(h), pl.ds(pl.multiple_of(part * 2 * width, 2 * width), 2 * width)
        )
        for copy in copies:
            copy.start()
        mine.start()
        return unused

    lax.fori_loop(0, halves * parts, head, 0)

    lag = RING - 1

    def units_of(k):
        def one(u, unused):
            g = k * UNITS + u
            gram(g)

            @pl.when(g >= 1)
            def _():
                pass_on(g - 1)

            @pl.when(g >= lag)
            def _():
                finish(g - lag)

            return unused

        lax.fori_loop(0, UNITS, one, 0)

    def main(k, unused):
        @pl.when(k < chunks)
        def _():
            @pl.when(k >= 2)
            def _():
                sent(k - 2)

            def some(j, unused):
                h, part = quarter(j)
                transform(k, h, part)
                return unused

            lax.fori_loop(0, halves * parts, some, 0)
            send_units(k)

        units_of(k - 1)
        return unused

    lax.fori_loop(1, chunks + 1, main, 0)

    def last(j, unused):
        finish(unit_count - lag + j)
        return unused

    lax.fori_loop(0, lag, last, 0)

    for k in range(max(chunks - 2, 0), chunks):
        sent(k)

    def drain(j, unused):
        g = unit_count - RING + j
        for s in range(1, times):
            zcopy(g, s).wait_send()
        out_copy(g).wait()
        return unused

    lax.fori_loop(0, RING, drain, 0)

    @pl.when(place < times - 1)
    def _():
        history_copy().wait_send()


def whole_call(voltages, filter_taps, table, cosine, sine):
    feeds, times = lax.axis_size("feed"), lax.axis_size("tm")
    inputs, sample_count = voltages.shape
    tap_count, fft_length = filter_taps.shape
    frames = sample_count // fft_length
    chunks, rows = table.shape[0], table.shape[1] // 2
    units = chunks * UNITS
    total = feeds * inputs
    kept = tap_count - 1
    vmem = pl.BlockSpec(memory_space=pltpu.VMEM)
    return pl.pallas_call(
        whole_kernel,
        out_shape=jax.ShapeDtypeStruct((units, total, total), jnp.float32),
        in_specs=[pl.BlockSpec(memory_space=pl.ANY), vmem, vmem, vmem, vmem],
        out_specs=pl.BlockSpec(memory_space=pl.ANY),
        scratch_shapes=[
            pltpu.VMEM((STAGES, HALF, (GROUP + kept) * fft_length), jnp.bfloat16),
            pltpu.VMEM((inputs, kept * fft_length), jnp.bfloat16),
            pltpu.VMEM((inputs, frames, fft_length), jnp.bfloat16),
            pltpu.VMEM((2, rows * PITCH, 128), jnp.float32),
            pltpu.VMEM((2, UNITS, feeds, times, inputs, 2 * frames), jnp.bfloat16),
            pltpu.VMEM((units, feeds, times, inputs, 2 * frames), jnp.bfloat16),
            pltpu.VMEM((RING, total, total), jnp.float32),
            pltpu.VMEM((2, total, total), jnp.float32),
            pltpu.VMEM((RING, times - 1, total + NOTE_ROWS, total), jnp.int16),
            pltpu.VMEM((units, times - 1, total + NOTE_ROWS, total), jnp.int16),
            pltpu.VMEM((units - DIRECT, total + NOTE_ROWS, total), jnp.int16),
            pltpu.SemaphoreType.DMA((STAGES,)),
            pltpu.SemaphoreType.DMA((2,)),
            pltpu.SemaphoreType.DMA((units, feeds)),
            pltpu.SemaphoreType.DMA((units, feeds)),
            pltpu.SemaphoreType.DMA((units,)),
            pltpu.SemaphoreType.DMA((units, times)),
            pltpu.SemaphoreType.DMA((units, times)),
            pltpu.SemaphoreType.DMA((units - DIRECT,)),
            pltpu.SemaphoreType.DMA((RING,)),
        ],
        compiler_params=pltpu.CompilerParams(
            vmem_limit_bytes=VMEM_WHOLE, collective_id=0, has_side_effects=True
        ),
        cost_estimate=pl.CostEstimate(
            flops=8 * inputs * sample_count * 512,
            bytes_accessed=4 * inputs * sample_count,
            transcendentals=0,
        ),
    )(voltages, filter_taps, table, cosine, sine)


def whole_fits(voltages, filter_taps, channel_flags, feeds, times):
    inputs, frames = voltages.shape[0], voltages.shape[1] // filter_taps.shape[1]
    kept = channel_flags.shape[0] // times
    rows = UNITS * feeds * times
    if times != 4 or inputs % HALF or feeds & (feeds - 1) or kept % UNITS or frames % 128:
        return False
    if kept < 2 * UNITS or frames < 2 * GROUP:
        return False
    spectra = 2 * inputs * 2 * frames
    total = feeds * inputs
    held = 2 * inputs * voltages.shape[1]
    held += spectra * (2 * rows + kept * feeds * times) + 1024 * rows * PITCH
    held += 2 * STAGES * HALF * (GROUP + 3) * filter_taps.shape[1]
    held += 2 * ((RING + kept) * (times - 1) + kept - DIRECT) * (total + NOTE_ROWS) * total
    held += 4 * (RING + 2) * total * total
    return held < VMEM_WHOLE - 3 * 1000 * 1000


def on_device_whole(voltages, filter_taps, delays, channel_flags):
    inputs = voltages.shape[0]
    fft_length = filter_taps.shape[1]
    feeds, times = lax.axis_size("feed"), lax.axis_size("tm")
    frame_total = voltages.shape[1] // fft_length * times
    owned = channel_flags.shape[0]
    kept = owned // times
    chunks = kept // UNITS
    order = np.arange(feeds * owned).reshape(feeds, times, chunks, UNITS)
    order = order.transpose(2, 3, 0, 1).reshape(chunks, -1)
    table = jnp.asarray(np.stack([table_rows(order[k], fft_length) for k in range(chunks)]))
    angles = 2.0 * math.pi / fft_length * jnp.asarray(order, jnp.float32)[:, None, :]
    angles = angles * delays[None, :, None]
    scale = 1.0 / math.sqrt(fft_length)
    shape = (chunks, inputs // HALF, HALF, order.shape[1])
    cosine = (jnp.cos(angles) * scale).reshape(shape)
    sine = (jnp.sin(angles) * scale).reshape(shape)
    vis = whole_call(voltages, filter_taps, table, cosine, sine)
    flags = lax.dynamic_slice_in_dim(channel_flags, lax.axis_index("tm") * kept, kept, 0)
    return vis * (flags.astype(jnp.float32) * (1.0 / frame_total))[:, None, None]


def on_device(voltages, filter_taps, delays, channel_flags):
    feeds, times = lax.axis_size("feed"), lax.axis_size("tm")
    if whole_fits(voltages, filter_taps, channel_flags, feeds, times):
        return on_device_whole(voltages, filter_taps, delays, channel_flags)
    return on_device_steps(voltages, filter_taps, delays, channel_flags)


def solution(mesh):
    in_specs = (P("feed", "tm"), P(), P("feed"), P("feed"))
    out_specs = P(("feed", "tm"), None, None)
    return jax.shard_map(
        on_device, mesh=mesh, in_specs=in_specs, out_specs=out_specs, check_vma=False
    )
```

```python
import functools
import math

import jax
import jax.numpy as jnp
import numpy as np
from jax import lax
from jax.experimental import pallas as pl
from jax.experimental.pallas import tpu as pltpu
from jax.sharding import PartitionSpec as P

VMEM_LIMIT = 56 * 1024 * 1024
SEND_PEAK = 16384.0
EXTRA_ROWS = 8


def passed_along(block, axis, distance):
    devices = range(lax.axis_size(axis))
    route = [(i - distance, i) for i in devices if i - distance in devices]
    return lax.ppermute(block, axis, route)


def table_rows(channels, fft_length):
    samples = np.arange(fft_length, dtype=np.int64)
    product = channels[:, None].astype(np.int64) * samples[None, :] % fft_length
    angles = product.astype(np.float32) * np.float32(2.0 * math.pi / fft_length)
    rows = np.concatenate([np.cos(angles), -np.sin(angles)], axis=0)
    return rows.astype(jnp.bfloat16)


def dft_kernel(table_ref, cos_ref, sin_ref, filtered_ref, out_ref, *turned):
    inputs, frames = filtered_ref.shape[0], filtered_ref.shape[1]
    rows = table_ref.shape[0] // 2
    width = 128
    for i in range(inputs):
        raw = lax.dot_general(
            table_ref[...], filtered_ref[i], (((1,), (1,)), ((), ())),
            preferred_element_type=jnp.float32,
        )
        real, imag = raw[:rows], raw[rows:]
        cosine = cos_ref[0, :, i : i + 1]
        sine = sin_ref[0, :, i : i + 1]
        both = (real * cosine + imag * sine, imag * cosine - real * sine)
        for q in range(2):
            for piece in range(frames // width):
                turned[q * (frames // width) + piece][pl.ds(i, rows, stride=inputs), :] = both[q][
                    :, piece * width : (piece + 1) * width
                ]
    for piece, ref in enumerate(turned):
        value = ref[...].reshape(rows, inputs, width).astype(jnp.bfloat16)
        out_ref[:, :, piece * width : (piece + 1) * width] = value


def dft_call(table, cosine, sine, filtered):
    blocks, rows, inputs = cosine.shape
    inputs_here, frames, fft_length = filtered.shape
    out_shape = jax.ShapeDtypeStruct((rows, inputs_here, 2 * frames), jnp.bfloat16)
    return pl.pallas_call(
        dft_kernel,
        out_shape=out_shape,
        grid=(blocks,),
        in_specs=[
            pl.BlockSpec((2 * rows, fft_length), lambda b: (0, 0)),
            pl.BlockSpec((1, rows, inputs), lambda b: (b, 0, 0)),
            pl.BlockSpec((1, rows, inputs), lambda b: (b, 0, 0)),
            pl.BlockSpec((inputs, frames, fft_length), lambda b: (b, 0, 0)),
        ],
        out_specs=pl.BlockSpec((rows, inputs, 2 * frames), lambda b: (0, b, 0)),
        scratch_shapes=[pltpu.VMEM((rows * inputs, 128), jnp.float32)] * (2 * frames // 128),
        compiler_params=pltpu.CompilerParams(vmem_limit_bytes=VMEM_LIMIT),
        cost_estimate=pl.CostEstimate(
            flops=10 * 4 * rows * inputs_here * frames * fft_length,
            bytes_accessed=2 * inputs_here * frames * (fft_length + 2 * rows),
            transcendentals=0,
        ),
    )(table, cosine, sine, filtered)


def gram_kernel(spectra_ref, vis_ref):
    sources, channels, inputs_here, columns = spectra_ref.shape
    total = sources * inputs_here
    half = columns // 2
    row = lax.broadcasted_iota(jnp.int32, (total, total), 0)
    column = lax.broadcasted_iota(jnp.int32, (total, total), 1)
    dims = (((1,), (1,)), ((), ()))
    for c in range(channels):
        slab = spectra_ref[:, c]
        if inputs_here % 16:
            slab = slab.astype(jnp.float32).reshape(total, columns).astype(jnp.bfloat16)
        else:
            slab = slab.reshape(total, columns)
        swapped = jnp.concatenate([slab[:, half:], -slab[:, :half]], axis=1)
        real = lax.dot_general(slab, slab, dims, preferred_element_type=jnp.float32)
        imag = lax.dot_general(swapped, slab, dims, preferred_element_type=jnp.float32)
        packed = jnp.where(row <= column, real, imag)
        peak = jnp.max(jnp.where(row == column, real, 0.0), axis=(0, 1), keepdims=True)
        peak = jnp.maximum(peak, 1e-30)
        power = jnp.ceil(jnp.log2(peak))
        vis_ref[c, :total] = packed * (SEND_PEAK * jnp.exp2(-power))
        vis_ref[c, total:] = jnp.broadcast_to(power, (EXTRA_ROWS, total))


def gram_call(spectra):
    sources, channels, inputs_here, columns = spectra.shape
    total = sources * inputs_here
    step = 2 if channels % 2 == 0 else 1
    return pl.pallas_call(
        gram_kernel,
        out_shape=jax.ShapeDtypeStruct((channels, total + EXTRA_ROWS, total), jnp.float32),
        grid=(channels // step,),
        in_specs=[pl.BlockSpec((sources, step, inputs_here, columns), lambda b: (0, b, 0, 0))],
        out_specs=pl.BlockSpec((step, total + EXTRA_ROWS, total), lambda b: (b, 0, 0)),
        compiler_params=pltpu.CompilerParams(vmem_limit_bytes=VMEM_LIMIT),
        cost_estimate=pl.CostEstimate(
            flops=40 * 4 * channels * total * total * columns,
            bytes_accessed=2 * channels * total * (columns + 2 * total),
            transcendentals=0,
        ),
    )(spectra)


def filter_kernel(history_ref, taps_ref, block_ref, out_ref, carry, turned):
    tap_count, fft_length = taps_ref.shape
    inputs, group = out_ref.shape[0], out_ref.shape[1]
    kept = tap_count - 1

    @pl.when(pl.program_id(0) == 0)
    def _():
        carry[...] = history_ref[...]

    def piece(p, unused):
        lanes = pl.multiple_of(p * 128, 128)
        taps = [taps_ref[t : t + 1, pl.ds(lanes, 128)] for t in range(tap_count)]
        frames = [
            carry[:, pl.ds(pl.multiple_of(h * fft_length + lanes, 128), 128)].astype(jnp.float32)
            for h in range(kept)
        ]
        for m in range(group):
            start = pl.multiple_of(m * fft_length + lanes, 128)
            frames.append(block_ref[:, pl.ds(start, 128)].astype(jnp.float32))
            value = taps[0] * frames[-1]
            for t in range(1, tap_count):
                value = value + taps[t] * frames[-1 - t]
            turned[pl.ds(m, inputs, stride=group), :] = value
        result = turned[...].reshape(inputs, group, 128).astype(jnp.bfloat16)
        out_ref[:, :, pl.ds(lanes, 128)] = result
        return unused

    lax.fori_loop(0, fft_length // 128, piece, 0)
    carry[...] = block_ref[:, (group - kept) * fft_length :]


def filter_frames(voltages, filter_taps):
    inputs_here, sample_count = voltages.shape
    tap_count, fft_length = filter_taps.shape
    frames = sample_count // fft_length
    kept = (tap_count - 1) * fft_length
    group = 16
    history = passed_along(voltages[:, sample_count - kept :], "tm", 1)
    return pl.pallas_call(
        filter_kernel,
        out_shape=jax.ShapeDtypeStruct((inputs_here, frames, fft_length), jnp.bfloat16),
        grid=(frames // group,),
        in_specs=[
            pl.BlockSpec((inputs_here, kept), lambda b: (0, 0)),
            pl.BlockSpec((tap_count, fft_length), lambda b: (0, 0)),
            pl.BlockSpec((inputs_here, group * fft_length), lambda b: (0, b)),
        ],
        out_specs=pl.BlockSpec((inputs_here, group, fft_length), lambda b: (0, b, 0)),
        scratch_shapes=[
            pltpu.VMEM((inputs_here, kept), jnp.bfloat16),
            pltpu.VMEM((inputs_here * group, 128), jnp.float32),
        ],
        compiler_params=pltpu.CompilerParams(vmem_limit_bytes=VMEM_LIMIT),
        cost_estimate=pl.CostEstimate(
            flops=8 * inputs_here * sample_count,
            bytes_accessed=4 * inputs_here * sample_count,
            transcendentals=0,
        ),
    )(history, filter_taps, voltages)


def on_device_steps(voltages, filter_taps, delays, channel_flags):
    inputs_here = voltages.shape[0]
    fft_length = filter_taps.shape[1]
    feeds, times = lax.axis_size("feed"), lax.axis_size("tm")
    filtered = filter_frames(voltages, filter_taps)
    frame_total = filtered.shape[1] * times
    owned = channel_flags.shape[0]
    kept = owned // times
    chunks = 4 if kept % 4 == 0 else 1
    width = kept // chunks
    block = 16 if inputs_here % 16 == 0 else inputs_here

    local_flags = lax.dynamic_slice_in_dim(
        channel_flags, lax.axis_index("tm") * kept, kept, 0
    ).astype(jnp.float32)
    flag_parts = (local_flags * (1.0 / (SEND_PEAK * frame_total))).reshape(chunks, width)
    scale = 1.0 / math.sqrt(fft_length)
    order = np.arange(feeds * owned).reshape(feeds, times, chunks, width)
    place = lax.axis_index("tm")

    def summed(vis, flags):
        total = 0.0
        for shift in range(times):
            target = lax.rem(place + shift, times)
            part = lax.dynamic_index_in_dim(vis, target, 0, keepdims=False)
            if shift:
                route = [(i, (i + shift) % times) for i in range(times)]
                part = lax.ppermute(part, "tm", route)
            part = part.astype(jnp.float32)
            count = part.shape[2]
            total = total + part[:, :count] * jnp.exp2(part[:, count:, :1][:, :1])
        return total * flags[:, None, None]

    results = []
    sent = []
    for k in range(chunks):
        channels = order[:, :, k].reshape(-1)
        table = jnp.asarray(table_rows(channels, fft_length))
        angles = 2.0 * math.pi / fft_length * jnp.asarray(channels, jnp.float32)[None, :, None]
        angles = angles * delays.reshape(-1, 1, block)
        if k >= 2:
            filtered, sent[k - 2] = lax.optimization_barrier((filtered, sent[k - 2]))
            results.append(summed(sent[k - 2], flag_parts[k - 2]))
        spectra = dft_call(table, jnp.cos(angles) * scale, jnp.sin(angles) * scale, filtered)
        spectra = spectra.reshape(feeds, times * width, inputs_here, spectra.shape[2])
        if k >= 3:
            spectra, results[k - 3] = lax.optimization_barrier((spectra, results[k - 3]))
        turned = lax.all_to_all(spectra, "feed", split_axis=0, concat_axis=0, tiled=True)
        if k >= 2:
            turned, results[k - 2] = lax.optimization_barrier((turned, results[k - 2]))
        vis = gram_call(turned).astype(jnp.float16)
        sent.append(vis.reshape(times, width, vis.shape[1], vis.shape[2]))
    for k in range(len(results), chunks):
        results.append(summed(sent[k], flag_parts[k]))
    return jnp.concatenate(results, axis=0)


VMEM_WHOLE = 64 * 1000 * 1000
MESH = pl.DeviceIdType.MESH
HALF = 16
GROUP = 16
UNITS = 4
EARLY = 2
LEVELS = 32760.0
NOTE_ROWS = 16
RING = 3
DIRECT = 1
ORDER = (3, 2, 1, 0)
STAGES = 4
PITCH = GROUP + 1


def whole_kernel(
    volt_ref, taps_ref, table_ref, slope_ref, delay_ref, out_ref,
    stage, history, filtered, turned, send, recv, own, far, zsend, zrecv, relay,
    stage_sem, history_sems, send_sem, recv_sem, self_sem, zsend_sem, zrecv_sem, relay_sem, out_sem,
    last_send_sem, last_recv_sem,
):
    feeds, times = lax.axis_size("feed"), lax.axis_size("tm")
    me, place = lax.axis_index("feed"), lax.axis_index("tm")
    inputs, sample_count = volt_ref.shape
    tap_count, fft_length = taps_ref.shape
    frames = sample_count // fft_length
    kept = tap_count - 1
    halves = inputs // HALF
    chunks = table_ref.shape[0]
    rows = table_ref.shape[1] // 2
    unit_count = chunks * UNITS
    relayed = relay.shape[0]
    total = feeds * inputs
    width = 128
    parts = frames // width
    part_groups = width // GROUP

    barrier = pltpu.get_barrier_semaphore()
    for s in range(1, feeds):
        pl.semaphore_signal(barrier, inc=1, device_id=(me ^ s, place), device_id_type=MESH)
    for s in range(1, times):
        other = lax.rem(place + s, times)
        pl.semaphore_signal(barrier, inc=1, device_id=(me, other), device_id_type=MESH)
    def history_copy():
        return pltpu.make_async_remote_copy(
            src_ref=volt_ref.at[:, pl.ds(sample_count - kept * fft_length, kept * fft_length)],
            dst_ref=history,
            send_sem=history_sems.at[0],
            recv_sem=history_sems.at[1],
            device_id=(me, place + 1),
            device_id_type=MESH,
        )

    head_steps = halves * parts * part_groups

    def quarter(j):
        return j // parts, parts - 1 - lax.rem(j, parts)

    def block_copies(n):
        h, part = quarter(n // part_groups)
        g = part * part_groups + lax.rem(lax.rem(n, part_groups) + 1, part_groups)
        slot = lax.rem(n, STAGES)
        at = half_rows(h)
        first = pl.multiple_of(jnp.maximum(g * GROUP - kept, 0) * fft_length, 128)
        later = pltpu.make_async_copy(
            volt_ref.at[at, pl.ds(first, (GROUP + kept) * fft_length)],
            stage.at[slot],
            stage_sem.at[slot],
        )
        start = pltpu.make_async_copy(
            volt_ref.at[at, pl.ds(0, GROUP * fft_length)],
            stage.at[slot, :, pl.ds(kept * fft_length, GROUP * fft_length)],
            stage_sem.at[slot],
        )
        return g, slot, later, start

    def block_start(n):
        g, _, later, start = block_copies(n)

        @pl.when(g > 0)
        def _():
            later.start()

        @pl.when(g == 0)
        def _():
            start.start()

    def filter_part(j):
        h, _ = quarter(j)

        def step_body(step, unused):
            n = j * part_groups + step

            @pl.when(n + STAGES - 1 < head_steps)
            def _():
                block_start(n + STAGES - 1)

            g, slot, later, start = block_copies(n)

            @pl.when(g > 0)
            def _():
                later.wait()

            @pl.when(g == 0)
            def _():
                start.wait()

                @pl.when(place == 0)
                def _():
                    stage[slot, :, : kept * fft_length] = jnp.zeros(
                        (HALF, kept * fft_length), jnp.bfloat16
                    )

                @pl.when(place > 0)
                def _():
                    @pl.when(h == 0)
                    def _():
                        history_copy().wait_recv()

                    stage[slot, :, : kept * fft_length] = history[half_rows(h), :]

            of = pl.ds(pl.multiple_of(g * GROUP, GROUP), GROUP)
            for lane in range(0, fft_length, width):
                taps = [taps_ref[t : t + 1, lane : lane + width] for t in range(tap_count)]

                def frame(j):
                    column = j * fft_length + lane
                    return stage[slot, :, column : column + width].astype(jnp.float32)

                window = [frame(j) for j in range(kept)]
                for m in range(GROUP):
                    window.append(frame(m + kept))
                    value = taps[0] * window[-1]
                    for t in range(1, tap_count):
                        value = value + taps[t] * window[-1 - t]
                    turned[0, pl.ds(m, HALF, stride=PITCH), :] = value
                for i in range(HALF):
                    rows_here = turned[0, i * PITCH : i * PITCH + GROUP]
                    filtered[h * HALF + i, of, lane : lane + width] = rows_here.astype(jnp.bfloat16)
            return unused

        lax.fori_loop(0, part_groups, step_body, 0)

    def transform(k, h, part):
        slot = lax.rem(k, 2)
        span = pl.ds(pl.multiple_of(part * width, width), width)
        block = filtered[half_rows(h), span].reshape(HALF * width, fft_length)
        raw = lax.dot_general(
            block, table_ref[k], (((1,), (1,)), ((), ())), preferred_element_type=jnp.float32
        )
        across = lax.broadcasted_iota(jnp.int32, (HALF, inputs), 1) - h * HALF
        mine = lax.broadcasted_iota(jnp.int32, (HALF, inputs), 0) == across
        delay = jnp.sum(jnp.where(mine, delay_ref[...], 0.0), axis=1, keepdims=True)
        angles = slope_ref[k] * delay
        scale = 1.0 / math.sqrt(fft_length)
        cosines, sines = jnp.cos(angles) * scale, jnp.sin(angles) * scale
        for i in range(HALF):
            here = raw[i * width : (i + 1) * width]
            real, imag = here[:, :rows], here[:, rows:]
            cosine = cosines[i : i + 1]
            sine = sines[i : i + 1]
            both = (real * cosine + imag * sine, imag * cosine - real * sine)
            for q in range(2):
                turned[q, pl.ds(i, rows, stride=PITCH), :] = jnp.transpose(both[q])
        for q in range(2):
            lanes = pl.ds(pl.multiple_of((2 * part + q) * width, width), width)
            for r in range(rows):
                u, f, t = r // (feeds * times), r // times % feeds, r % times
                value = turned[q, r * PITCH : r * PITCH + HALF].astype(jnp.bfloat16)
                send[slot, u, f, t, half_rows(h), lanes] = value

    def half_rows(h):
        return pl.ds(pl.multiple_of(h * HALF, HALF), HALF)

    def head_copies(at, lanes):
        copies = []
        for s in range(1, feeds):
            peer = me ^ s
            copies.append(
                pltpu.make_async_remote_copy(
                    src_ref=send.at[0, pl.ds(0, EARLY), peer, :, at, lanes],
                    dst_ref=recv.at[pl.ds(0, EARLY), me, :, at, lanes],
                    send_sem=send_sem.at[0, s],
                    recv_sem=recv_sem.at[0, s],
                    device_id=(peer, place),
                    device_id_type=MESH,
                )
            )
        mine = pltpu.make_async_copy(
            send.at[0, pl.ds(0, EARLY), me, :, at, lanes],
            recv.at[pl.ds(0, EARLY), me, :, at, lanes],
            self_sem.at[0],
        )
        return copies, mine

    def unit_copies(k, u):
        slot = lax.rem(k, 2)
        g = k * UNITS + u
        copies = []
        for s in range(1, feeds):
            peer = me ^ s
            copies.append(
                pltpu.make_async_remote_copy(
                    src_ref=send.at[slot, u, peer],
                    dst_ref=recv.at[g, me],
                    send_sem=send_sem.at[g, s],
                    recv_sem=recv_sem.at[g, s],
                    device_id=(peer, place),
                    device_id_type=MESH,
                )
            )
        mine = pltpu.make_async_copy(send.at[slot, u, me], recv.at[g, me], self_sem.at[g])
        return copies, mine

    all_rows, all_lanes = pl.ds(0, inputs), pl.ds(0, 2 * frames)
    last_unit = unit_count - 1

    def last_copies(j):
        copies = []
        channel = place ^ j
        for s in range(1, feeds):
            peer = me ^ s
            copies.append(
                pltpu.make_async_remote_copy(
                    src_ref=send.at[(chunks - 1) % 2, UNITS - 1, peer, channel],
                    dst_ref=recv.at[last_unit, me, channel],
                    send_sem=last_send_sem.at[j, s],
                    recv_sem=last_recv_sem.at[j, s],
                    device_id=(peer, place),
                    device_id_type=MESH,
                )
            )
        return copies

    def send_units(k, first):
        def one(u, unused):
            copies, mine = unit_copies(k, u)
            mine.start()

            @pl.when(k * UNITS + u < last_unit)
            def _():
                for copy in copies:
                    copy.start()

            @pl.when(k * UNITS + u == last_unit)
            def _():
                for j in ORDER:
                    for copy in last_copies(j):
                        copy.start()

            return unused

        lax.fori_loop(first, UNITS, one, 0)

    def sent(k):
        @pl.when(k == 0)
        def _():
            copies, _ = head_copies(all_rows, all_lanes)
            for copy in copies:
                copy.wait_send()

        def one(u, unused):
            g = k * UNITS + u

            @pl.when(jnp.logical_and(g >= EARLY, g < last_unit))
            def _():
                copies, _ = unit_copies(k, u)
                for copy in copies:
                    copy.wait_send()

            @pl.when(g == last_unit)
            def _():
                for j in ORDER:
                    for copy in last_copies(j):
                        copy.wait_send()

            return unused

        lax.fori_loop(0, UNITS, one, 0)

    def arrived(g):
        @pl.when(g == 0)
        def _():
            copies, mine = head_copies(all_rows, all_lanes)
            for copy in copies:
                copy.wait_recv()
            mine.wait()

        @pl.when(g >= EARLY)
        def _():
            copies, mine = unit_copies(g // UNITS, lax.rem(g, UNITS))
            mine.wait()

            @pl.when(g < last_unit)
            def _():
                for copy in copies:
                    copy.wait_recv()

    row = lax.broadcasted_iota(jnp.int32, (total, total), 0)
    column = lax.broadcasted_iota(jnp.int32, (total, total), 1)
    dims = (((1,), (1,)), ((), ()))

    middle = jnp.logical_and(place > 0, place < times - 1)

    def zcopy(g, s):
        return pltpu.make_async_remote_copy(
            src_ref=zsend.at[lax.rem(g, RING), s - 1],
            dst_ref=zrecv.at[g, s - 1],
            send_sem=zsend_sem.at[g, s],
            recv_sem=zrecv_sem.at[g, s],
            device_id=(me, place ^ s),
            device_id_type=MESH,
        )

    def relay_copy(g):
        return pltpu.make_async_remote_copy(
            src_ref=zsend.at[lax.rem(g, RING), 2],
            dst_ref=relay.at[g],
            send_sem=zsend_sem.at[g, 3],
            recv_sem=relay_sem.at[g],
            device_id=(me, place ^ 1),
            device_id_type=MESH,
        )

    def out_copy(g):
        slot = lax.rem(g, RING)
        return pltpu.make_async_copy(own.at[slot], out_ref.at[g], out_sem.at[slot])

    def gram(g):
        arrived(g)
        slot = lax.rem(g, RING)

        @pl.when(g >= RING)
        def _():
            for s in range(1, times):
                zcopy(g - RING, s).wait_send()
            out_copy(g - RING).wait()

        for s in ORDER:
            @pl.when(g == last_unit)
            def _():
                for copy in last_copies(s):
                    copy.wait_recv()

            slab = recv[g, :, place ^ s].reshape(total, 2 * frames)
            columns = [slab[:, j * width : (j + 1) * width] for j in range(2 * parts)]
            swapped = [-columns[j - 1] if j % 2 else columns[j + 1] for j in range(2 * parts)]
            swapped = jnp.concatenate(swapped, axis=1)
            real = lax.dot_general(slab, slab, dims, preferred_element_type=jnp.float32)
            imag = lax.dot_general(swapped, slab, dims, preferred_element_type=jnp.float32)
            packed = jnp.where(row <= column, real, imag)
            if s == 0:
                own[slot] = packed
            elif s == 1:
                code(packed, slot, s)
                zcopy(g, s).start()
            elif s == 3:
                code(packed, slot, s)
                passed_on = jnp.logical_and(jnp.logical_not(middle), g < relayed)

                @pl.when(passed_on)
                def _():
                    relay_copy(g).start()

                @pl.when(jnp.logical_not(passed_on))
                def _():
                    zcopy(g, s).start()
            else:
                held_back = jnp.logical_and(middle, g < relayed)

                @pl.when(held_back)
                def _():
                    far[lax.rem(g, 2)] = packed

                @pl.when(jnp.logical_not(held_back))
                def _():
                    code(packed, slot, s)
                    zcopy(g, s).start()

    def code(packed, slot, s):
        diagonal = jnp.where(row == column, packed, 0.0)
        powers = [
            jnp.ceil(0.5 * jnp.log2(jnp.maximum(jnp.sum(diagonal, axis=a, keepdims=True), 1e-30)))
            for a in range(2)
        ]
        scaled = packed * (LEVELS * jnp.exp2(-powers[0])) * jnp.exp2(-powers[1])
        zsend[slot, s - 1, :total] = jnp.round(scaled).astype(jnp.int32).astype(jnp.int16)
        note = jnp.broadcast_to(powers[0], (NOTE_ROWS, total))
        zsend[slot, s - 1, total:] = note.astype(jnp.int32).astype(jnp.int16)

    def decoded(value, note):
        across = jnp.exp2(note.astype(jnp.int32).astype(jnp.float32))[:1]
        down = jnp.sum(jnp.where(row == column, across, 0.0), axis=1, keepdims=True)
        return value.astype(jnp.int32).astype(jnp.float32) * across * (down * (1.0 / LEVELS))

    def pass_on(g):
        @pl.when(jnp.logical_and(middle, g < relayed))
        def _():
            relay_copy(g).wait_recv()
            both = far[lax.rem(g, 2)] + decoded(relay[g, :total], relay[g, total:])
            code(both, lax.rem(g, RING), 2)
            zcopy(g, 2).start()

    def finish(g):
        slot = lax.rem(g, RING)
        for s in (1, 2):
            zcopy(g, s).wait_recv()
            own[slot] += decoded(zrecv[g, s - 1, :total], zrecv[g, s - 1, total:])

        @pl.when(jnp.logical_or(middle, g >= relayed))
        def _():
            zcopy(g, 3).wait_recv()
            own[slot] += decoded(zrecv[g, 2, :total], zrecv[g, 2, total:])

        out_copy(g).start()

    for n in range(STAGES - 1):
        block_start(jnp.int32(n))

    def head(j, unused):
        h, part = quarter(j)
        filter_part(j)

        transform(0, h, part)

        @pl.when(j == 0)
        def _():
            pl.semaphore_wait(barrier, feeds + times - 2)

            @pl.when(place < times - 1)
            def _():
                history_copy().start()

        copies, mine = head_copies(
            half_rows(h), pl.ds(pl.multiple_of(part * 2 * width, 2 * width), 2 * width)
        )
        for copy in copies:
            copy.start()
        mine.start()
        return unused

    lax.fori_loop(0, halves * parts, head, 0)
    send_units(jnp.int32(0), EARLY)

    lag = RING - 1

    def units_of(k):
        def one(u, unused):
            g = k * UNITS + u

            @pl.when(g >= 1)
            def _():
                pass_on(g - 1)

            @pl.when(g >= lag)
            def _():
                finish(g - lag)

            gram(g)

            return unused

        lax.fori_loop(0, UNITS, one, 0)

    def main(k, unused):
        @pl.when(k < chunks)
        def _():
            @pl.when(k >= 2)
            def _():
                sent(k - 2)

            def some(j, unused):
                h, part = quarter(j)
                transform(k, h, part)
                return unused

            lax.fori_loop(0, halves * parts, some, 0)
            send_units(k, 0)

        units_of(k - 1)
        return unused

    lax.fori_loop(1, chunks + 1, main, 0)

    def last(j, unused):
        finish(unit_count - lag + j)
        return unused

    lax.fori_loop(0, lag, last, 0)

    for k in range(max(chunks - 2, 0), chunks):
        sent(k)

    def drain(j, unused):
        g = unit_count - RING + j
        for s in range(1, times):
            zcopy(g, s).wait_send()
        out_copy(g).wait()
        return unused

    lax.fori_loop(0, RING, drain, 0)

    @pl.when(place < times - 1)
    def _():
        history_copy().wait_send()


def whole_call(voltages, filter_taps, table, slopes, delays):
    feeds, times = lax.axis_size("feed"), lax.axis_size("tm")
    inputs, sample_count = voltages.shape
    tap_count, fft_length = filter_taps.shape
    frames = sample_count // fft_length
    chunks, rows = table.shape[0], table.shape[1] // 2
    units = chunks * UNITS
    total = feeds * inputs
    kept = tap_count - 1
    vmem = pl.BlockSpec(memory_space=pltpu.VMEM)
    return pl.pallas_call(
        whole_kernel,
        out_shape=jax.ShapeDtypeStruct((units, total, total), jnp.float32),
        in_specs=[pl.BlockSpec(memory_space=pl.ANY), vmem, vmem, vmem, vmem],
        out_specs=pl.BlockSpec(memory_space=pl.ANY),
        scratch_shapes=[
            pltpu.VMEM((STAGES, HALF, (GROUP + kept) * fft_length), jnp.bfloat16),
            pltpu.VMEM((inputs, kept * fft_length), jnp.bfloat16),
            pltpu.VMEM((inputs, frames, fft_length), jnp.bfloat16),
            pltpu.VMEM((2, rows * PITCH, 128), jnp.float32),
            pltpu.VMEM((2, UNITS, feeds, times, inputs, 2 * frames), jnp.bfloat16),
            pltpu.VMEM((units, feeds, times, inputs, 2 * frames), jnp.bfloat16),
            pltpu.VMEM((RING, total, total), jnp.float32),
            pltpu.VMEM((2, total, total), jnp.float32),
            pltpu.VMEM((RING, times - 1, total + NOTE_ROWS, total), jnp.int16),
            pltpu.VMEM((units, times - 1, total + NOTE_ROWS, total), jnp.int16),
            pltpu.VMEM((units - DIRECT, total + NOTE_ROWS, total), jnp.int16),
            pltpu.SemaphoreType.DMA((STAGES,)),
            pltpu.SemaphoreType.DMA((2,)),
            pltpu.SemaphoreType.DMA((units, feeds)),
            pltpu.SemaphoreType.DMA((units, feeds)),
            pltpu.SemaphoreType.DMA((units,)),
            pltpu.SemaphoreType.DMA((units, times)),
            pltpu.SemaphoreType.DMA((units, times)),
            pltpu.SemaphoreType.DMA((units - DIRECT,)),
            pltpu.SemaphoreType.DMA((RING,)),
            pltpu.SemaphoreType.DMA((times, feeds)),
            pltpu.SemaphoreType.DMA((times, feeds)),
        ],
        compiler_params=pltpu.CompilerParams(
            vmem_limit_bytes=VMEM_WHOLE, collective_id=0, has_side_effects=True
        ),
        cost_estimate=pl.CostEstimate(
            flops=8 * inputs * sample_count * 512,
            bytes_accessed=4 * inputs * sample_count,
            transcendentals=0,
        ),
    )(voltages, filter_taps, table, slopes, delays)


def whole_fits(voltages, filter_taps, channel_flags, feeds, times):
    inputs, frames = voltages.shape[0], voltages.shape[1] // filter_taps.shape[1]
    kept = channel_flags.shape[0] // times
    rows = UNITS * feeds * times
    if times != 4 or inputs % HALF or feeds & (feeds - 1) or kept % UNITS or frames % 128:
        return False
    if kept < 2 * UNITS or frames < 2 * GROUP:
        return False
    spectra = 2 * inputs * 2 * frames
    total = feeds * inputs
    held = 2 * inputs * voltages.shape[1]
    held += spectra * (2 * rows + kept * feeds * times) + 1024 * rows * PITCH
    held += 2 * STAGES * HALF * (GROUP + 3) * filter_taps.shape[1]
    held += 2 * ((RING + kept) * (times - 1) + kept - DIRECT) * (total + NOTE_ROWS) * total
    held += 4 * (RING + 2) * total * total
    return held < VMEM_WHOLE - 3 * 1000 * 1000


def on_device_whole(voltages, filter_taps, delays, channel_flags):
    inputs = voltages.shape[0]
    fft_length = filter_taps.shape[1]
    feeds, times = lax.axis_size("feed"), lax.axis_size("tm")
    frame_total = voltages.shape[1] // fft_length * times
    owned = channel_flags.shape[0]
    kept = owned // times
    chunks = kept // UNITS
    order = np.arange(feeds * owned).reshape(feeds, times, chunks, UNITS)
    order = order.transpose(2, 3, 0, 1).reshape(chunks, -1)
    table = jnp.asarray(np.stack([table_rows(order[k], fft_length) for k in range(chunks)]))
    slopes = np.float32(2.0 * math.pi / fft_length) * order.astype(np.float32)
    slopes = jnp.asarray(slopes[:, None, :])
    vis = whole_call(voltages, filter_taps, table, slopes, delays.reshape(1, inputs))
    flags = lax.dynamic_slice_in_dim(channel_flags, lax.axis_index("tm") * kept, kept, 0)
    return vis * (flags.astype(jnp.float32) * (1.0 / frame_total))[:, None, None]


def on_device(voltages, filter_taps, delays, channel_flags):
    feeds, times = lax.axis_size("feed"), lax.axis_size("tm")
    if whole_fits(voltages, filter_taps, channel_flags, feeds, times):
        return on_device_whole(voltages, filter_taps, delays, channel_flags)
    return on_device_steps(voltages, filter_taps, delays, channel_flags)


def solution(mesh):
    in_specs = (P("feed", "tm"), P(), P("feed"), P("feed"))
    out_specs = P(("feed", "tm"), None, None)
    return jax.shard_map(
        on_device, mesh=mesh, in_specs=in_specs, out_specs=out_specs, check_vma=False
    )
```

```python
import functools
import math

import jax
import jax.numpy as jnp
import numpy as np
from jax import lax
from jax.experimental import pallas as pl
from jax.experimental.pallas import tpu as pltpu
from jax.sharding import PartitionSpec as P

VMEM_LIMIT = 56 * 1024 * 1024
SEND_PEAK = 16384.0
EXTRA_ROWS = 8


def passed_along(block, axis, distance):
    devices = range(lax.axis_size(axis))
    route = [(i - distance, i) for i in devices if i - distance in devices]
    return lax.ppermute(block, axis, route)


def table_rows(channels, fft_length):
    samples = np.arange(fft_length, dtype=np.int64)
    product = channels[:, None].astype(np.int64) * samples[None, :] % fft_length
    angles = product.astype(np.float32) * np.float32(2.0 * math.pi / fft_length)
    rows = np.concatenate([np.cos(angles), -np.sin(angles)], axis=0)
    return rows.astype(jnp.bfloat16)


def dft_kernel(table_ref, cos_ref, sin_ref, filtered_ref, out_ref, *turned):
    inputs, frames = filtered_ref.shape[0], filtered_ref.shape[1]
    rows = table_ref.shape[0] // 2
    width = 128
    for i in range(inputs):
        raw = lax.dot_general(
            table_ref[...], filtered_ref[i], (((1,), (1,)), ((), ())),
            preferred_element_type=jnp.float32,
        )
        real, imag = raw[:rows], raw[rows:]
        cosine = cos_ref[0, :, i : i + 1]
        sine = sin_ref[0, :, i : i + 1]
        both = (real * cosine + imag * sine, imag * cosine - real * sine)
        for q in range(2):
            for piece in range(frames // width):
                turned[q * (frames // width) + piece][pl.ds(i, rows, stride=inputs), :] = both[q][
                    :, piece * width : (piece + 1) * width
                ]
    for piece, ref in enumerate(turned):
        value = ref[...].reshape(rows, inputs, width).astype(jnp.bfloat16)
        out_ref[:, :, piece * width : (piece + 1) * width] = value


def dft_call(table, cosine, sine, filtered):
    blocks, rows, inputs = cosine.shape
    inputs_here, frames, fft_length = filtered.shape
    out_shape = jax.ShapeDtypeStruct((rows, inputs_here, 2 * frames), jnp.bfloat16)
    return pl.pallas_call(
        dft_kernel,
        out_shape=out_shape,
        grid=(blocks,),
        in_specs=[
            pl.BlockSpec((2 * rows, fft_length), lambda b: (0, 0)),
            pl.BlockSpec((1, rows, inputs), lambda b: (b, 0, 0)),
            pl.BlockSpec((1, rows, inputs), lambda b: (b, 0, 0)),
            pl.BlockSpec((inputs, frames, fft_length), lambda b: (b, 0, 0)),
        ],
        out_specs=pl.BlockSpec((rows, inputs, 2 * frames), lambda b: (0, b, 0)),
        scratch_shapes=[pltpu.VMEM((rows * inputs, 128), jnp.float32)] * (2 * frames // 128),
        compiler_params=pltpu.CompilerParams(vmem_limit_bytes=VMEM_LIMIT),
        cost_estimate=pl.CostEstimate(
            flops=10 * 4 * rows * inputs_here * frames * fft_length,
            bytes_accessed=2 * inputs_here * frames * (fft_length + 2 * rows),
            transcendentals=0,
        ),
    )(table, cosine, sine, filtered)


def gram_kernel(spectra_ref, vis_ref):
    sources, channels, inputs_here, columns = spectra_ref.shape
    total = sources * inputs_here
    half = columns // 2
    row = lax.broadcasted_iota(jnp.int32, (total, total), 0)
    column = lax.broadcasted_iota(jnp.int32, (total, total), 1)
    dims = (((1,), (1,)), ((), ()))
    for c in range(channels):
        slab = spectra_ref[:, c]
        if inputs_here % 16:
            slab = slab.astype(jnp.float32).reshape(total, columns).astype(jnp.bfloat16)
        else:
            slab = slab.reshape(total, columns)
        swapped = jnp.concatenate([slab[:, half:], -slab[:, :half]], axis=1)
        real = lax.dot_general(slab, slab, dims, preferred_element_type=jnp.float32)
        imag = lax.dot_general(swapped, slab, dims, preferred_element_type=jnp.float32)
        packed = jnp.where(row <= column, real, imag)
        peak = jnp.max(jnp.where(row == column, real, 0.0), axis=(0, 1), keepdims=True)
        peak = jnp.maximum(peak, 1e-30)
        power = jnp.ceil(jnp.log2(peak))
        vis_ref[c, :total] = packed * (SEND_PEAK * jnp.exp2(-power))
        vis_ref[c, total:] = jnp.broadcast_to(power, (EXTRA_ROWS, total))


def gram_call(spectra):
    sources, channels, inputs_here, columns = spectra.shape
    total = sources * inputs_here
    step = 2 if channels % 2 == 0 else 1
    return pl.pallas_call(
        gram_kernel,
        out_shape=jax.ShapeDtypeStruct((channels, total + EXTRA_ROWS, total), jnp.float32),
        grid=(channels // step,),
        in_specs=[pl.BlockSpec((sources, step, inputs_here, columns), lambda b: (0, b, 0, 0))],
        out_specs=pl.BlockSpec((step, total + EXTRA_ROWS, total), lambda b: (b, 0, 0)),
        compiler_params=pltpu.CompilerParams(vmem_limit_bytes=VMEM_LIMIT),
        cost_estimate=pl.CostEstimate(
            flops=40 * 4 * channels * total * total * columns,
            bytes_accessed=2 * channels * total * (columns + 2 * total),
            transcendentals=0,
        ),
    )(spectra)


def filter_kernel(history_ref, taps_ref, block_ref, out_ref, carry, turned):
    tap_count, fft_length = taps_ref.shape
    inputs, group = out_ref.shape[0], out_ref.shape[1]
    kept = tap_count - 1

    @pl.when(pl.program_id(0) == 0)
    def _():
        carry[...] = history_ref[...]

    def piece(p, unused):
        lanes = pl.multiple_of(p * 128, 128)
        taps = [taps_ref[t : t + 1, pl.ds(lanes, 128)] for t in range(tap_count)]
        frames = [
            carry[:, pl.ds(pl.multiple_of(h * fft_length + lanes, 128), 128)].astype(jnp.float32)
            for h in range(kept)
        ]
        for m in range(group):
            start = pl.multiple_of(m * fft_length + lanes, 128)
            frames.append(block_ref[:, pl.ds(start, 128)].astype(jnp.float32))
            value = taps[0] * frames[-1]
            for t in range(1, tap_count):
                value = value + taps[t] * frames[-1 - t]
            turned[pl.ds(m, inputs, stride=group), :] = value
        result = turned[...].reshape(inputs, group, 128).astype(jnp.bfloat16)
        out_ref[:, :, pl.ds(lanes, 128)] = result
        return unused

    lax.fori_loop(0, fft_length // 128, piece, 0)
    carry[...] = block_ref[:, (group - kept) * fft_length :]


def filter_frames(voltages, filter_taps):
    inputs_here, sample_count = voltages.shape
    tap_count, fft_length = filter_taps.shape
    frames = sample_count // fft_length
    kept = (tap_count - 1) * fft_length
    group = 16
    history = passed_along(voltages[:, sample_count - kept :], "tm", 1)
    return pl.pallas_call(
        filter_kernel,
        out_shape=jax.ShapeDtypeStruct((inputs_here, frames, fft_length), jnp.bfloat16),
        grid=(frames // group,),
        in_specs=[
            pl.BlockSpec((inputs_here, kept), lambda b: (0, 0)),
            pl.BlockSpec((tap_count, fft_length), lambda b: (0, 0)),
            pl.BlockSpec((inputs_here, group * fft_length), lambda b: (0, b)),
        ],
        out_specs=pl.BlockSpec((inputs_here, group, fft_length), lambda b: (0, b, 0)),
        scratch_shapes=[
            pltpu.VMEM((inputs_here, kept), jnp.bfloat16),
            pltpu.VMEM((inputs_here * group, 128), jnp.float32),
        ],
        compiler_params=pltpu.CompilerParams(vmem_limit_bytes=VMEM_LIMIT),
        cost_estimate=pl.CostEstimate(
            flops=8 * inputs_here * sample_count,
            bytes_accessed=4 * inputs_here * sample_count,
            transcendentals=0,
        ),
    )(history, filter_taps, voltages)


def on_device_steps(voltages, filter_taps, delays, channel_flags):
    inputs_here = voltages.shape[0]
    fft_length = filter_taps.shape[1]
    feeds, times = lax.axis_size("feed"), lax.axis_size("tm")
    filtered = filter_frames(voltages, filter_taps)
    frame_total = filtered.shape[1] * times
    owned = channel_flags.shape[0]
    kept = owned // times
    chunks = 4 if kept % 4 == 0 else 1
    width = kept // chunks
    block = 16 if inputs_here % 16 == 0 else inputs_here

    local_flags = lax.dynamic_slice_in_dim(
        channel_flags, lax.axis_index("tm") * kept, kept, 0
    ).astype(jnp.float32)
    flag_parts = (local_flags * (1.0 / (SEND_PEAK * frame_total))).reshape(chunks, width)
    scale = 1.0 / math.sqrt(fft_length)
    order = np.arange(feeds * owned).reshape(feeds, times, chunks, width)
    place = lax.axis_index("tm")

    def summed(vis, flags):
        total = 0.0
        for shift in range(times):
            target = lax.rem(place + shift, times)
            part = lax.dynamic_index_in_dim(vis, target, 0, keepdims=False)
            if shift:
                route = [(i, (i + shift) % times) for i in range(times)]
                part = lax.ppermute(part, "tm", route)
            part = part.astype(jnp.float32)
            count = part.shape[2]
            total = total + part[:, :count] * jnp.exp2(part[:, count:, :1][:, :1])
        return total * flags[:, None, None]

    results = []
    sent = []
    for k in range(chunks):
        channels = order[:, :, k].reshape(-1)
        table = jnp.asarray(table_rows(channels, fft_length))
        angles = 2.0 * math.pi / fft_length * jnp.asarray(channels, jnp.float32)[None, :, None]
        angles = angles * delays.reshape(-1, 1, block)
        if k >= 2:
            filtered, sent[k - 2] = lax.optimization_barrier((filtered, sent[k - 2]))
            results.append(summed(sent[k - 2], flag_parts[k - 2]))
        spectra = dft_call(table, jnp.cos(angles) * scale, jnp.sin(angles) * scale, filtered)
        spectra = spectra.reshape(feeds, times * width, inputs_here, spectra.shape[2])
        if k >= 3:
            spectra, results[k - 3] = lax.optimization_barrier((spectra, results[k - 3]))
        turned = lax.all_to_all(spectra, "feed", split_axis=0, concat_axis=0, tiled=True)
        if k >= 2:
            turned, results[k - 2] = lax.optimization_barrier((turned, results[k - 2]))
        vis = gram_call(turned).astype(jnp.float16)
        sent.append(vis.reshape(times, width, vis.shape[1], vis.shape[2]))
    for k in range(len(results), chunks):
        results.append(summed(sent[k], flag_parts[k]))
    return jnp.concatenate(results, axis=0)


VMEM_WHOLE = 64 * 1000 * 1000
MESH = pl.DeviceIdType.MESH
HALF = 16
GROUP = 16
UNITS = 4
EARLY = 3
LEVELS = 32760.0
NOTE_ROWS = 16
RING = 3
DIRECT = 1
ORDER = (3, 2, 1, 0)
STAGES = 4
PITCH = GROUP + 1


def whole_kernel(
    volt_ref, taps_ref, table_ref, slope_ref, delay_ref, out_ref,
    stage, history, filtered, turned, send, recv, own, far, zsend, zrecv, relay,
    stage_sem, history_sems, send_sem, recv_sem, self_sem, zsend_sem, zrecv_sem, relay_sem, out_sem,
    last_send_sem, last_recv_sem,
):
    feeds, times = lax.axis_size("feed"), lax.axis_size("tm")
    me, place = lax.axis_index("feed"), lax.axis_index("tm")
    inputs, sample_count = volt_ref.shape
    tap_count, fft_length = taps_ref.shape
    frames = sample_count // fft_length
    kept = tap_count - 1
    halves = inputs // HALF
    chunks = table_ref.shape[0]
    rows = table_ref.shape[1] // 2
    unit_count = chunks * UNITS
    relayed = relay.shape[0]
    total = feeds * inputs
    width = 128
    parts = frames // width
    part_groups = width // GROUP

    barrier = pltpu.get_barrier_semaphore()
    for s in range(1, feeds):
        pl.semaphore_signal(barrier, inc=1, device_id=(me ^ s, place), device_id_type=MESH)
    for s in range(1, times):
        other = lax.rem(place + s, times)
        pl.semaphore_signal(barrier, inc=1, device_id=(me, other), device_id_type=MESH)
    def history_copy():
        return pltpu.make_async_remote_copy(
            src_ref=volt_ref.at[:, pl.ds(sample_count - kept * fft_length, kept * fft_length)],
            dst_ref=history,
            send_sem=history_sems.at[0],
            recv_sem=history_sems.at[1],
            device_id=(me, place + 1),
            device_id_type=MESH,
        )

    head_steps = halves * parts * part_groups

    def quarter(j):
        return j // parts, parts - 1 - lax.rem(j, parts)

    def block_copies(n):
        h, part = quarter(n // part_groups)
        g = part * part_groups + lax.rem(lax.rem(n, part_groups) + 1, part_groups)
        slot = lax.rem(n, STAGES)
        at = half_rows(h)
        first = pl.multiple_of(jnp.maximum(g * GROUP - kept, 0) * fft_length, 128)
        later = pltpu.make_async_copy(
            volt_ref.at[at, pl.ds(first, (GROUP + kept) * fft_length)],
            stage.at[slot],
            stage_sem.at[slot],
        )
        start = pltpu.make_async_copy(
            volt_ref.at[at, pl.ds(0, GROUP * fft_length)],
            stage.at[slot, :, pl.ds(kept * fft_length, GROUP * fft_length)],
            stage_sem.at[slot],
        )
        return g, slot, later, start

    def block_start(n):
        g, _, later, start = block_copies(n)

        @pl.when(g > 0)
        def _():
            later.start()

        @pl.when(g == 0)
        def _():
            start.start()

    def filter_part(j):
        h, _ = quarter(j)

        def step_body(step, unused):
            n = j * part_groups + step

            @pl.when(n + STAGES - 1 < head_steps)
            def _():
                block_start(n + STAGES - 1)

            g, slot, later, start = block_copies(n)

            @pl.when(g > 0)
            def _():
                later.wait()

            @pl.when(g == 0)
            def _():
                start.wait()

                @pl.when(place == 0)
                def _():
                    stage[slot, :, : kept * fft_length] = jnp.zeros(
                        (HALF, kept * fft_length), jnp.bfloat16
                    )

                @pl.when(place > 0)
                def _():
                    @pl.when(h == 0)
                    def _():
                        history_copy().wait_recv()

                    stage[slot, :, : kept * fft_length] = history[half_rows(h), :]

            of = pl.ds(pl.multiple_of(g * GROUP, GROUP), GROUP)
            for lane in range(0, fft_length, width):
                taps = [taps_ref[t : t + 1, lane : lane + width] for t in range(tap_count)]

                def frame(j):
                    column = j * fft_length + lane
                    return stage[slot, :, column : column + width].astype(jnp.float32)

                window = [frame(j) for j in range(kept)]
                for m in range(GROUP):
                    window.append(frame(m + kept))
                    value = taps[0] * window[-1]
                    for t in range(1, tap_count):
                        value = value + taps[t] * window[-1 - t]
                    turned[0, pl.ds(m, HALF, stride=PITCH), :] = value
                for i in range(HALF):
                    rows_here = turned[0, i * PITCH : i * PITCH + GROUP]
                    filtered[h * HALF + i, of, lane : lane + width] = rows_here.astype(jnp.bfloat16)
            return unused

        lax.fori_loop(0, part_groups, step_body, 0)

    def transform(k, h, part):
        slot = lax.rem(k, 2)
        span = pl.ds(pl.multiple_of(part * width, width), width)
        block = filtered[half_rows(h), span].reshape(HALF * width, fft_length)
        raw = lax.dot_general(
            block, table_ref[k], (((1,), (1,)), ((), ())), preferred_element_type=jnp.float32
        )
        across = lax.broadcasted_iota(jnp.int32, (HALF, inputs), 1) - h * HALF
        mine = lax.broadcasted_iota(jnp.int32, (HALF, inputs), 0) == across
        delay = jnp.sum(jnp.where(mine, delay_ref[...], 0.0), axis=1, keepdims=True)
        angles = slope_ref[k] * delay
        scale = 1.0 / math.sqrt(fft_length)
        cosines, sines = jnp.cos(angles) * scale, jnp.sin(angles) * scale
        for i in range(HALF):
            here = raw[i * width : (i + 1) * width]
            real, imag = here[:, :rows], here[:, rows:]
            cosine = cosines[i : i + 1]
            sine = sines[i : i + 1]
            both = (real * cosine + imag * sine, imag * cosine - real * sine)
            for q in range(2):
                turned[q, pl.ds(i, rows, stride=PITCH), :] = jnp.transpose(both[q])
        for q in range(2):
            lanes = pl.ds(pl.multiple_of((2 * part + q) * width, width), width)
            for r in range(rows):
                u, f, t = r // (feeds * times), r // times % feeds, r % times
                value = turned[q, r * PITCH : r * PITCH + HALF].astype(jnp.bfloat16)
                send[slot, u, f, t, half_rows(h), lanes] = value

    def half_rows(h):
        return pl.ds(pl.multiple_of(h * HALF, HALF), HALF)

    def head_copies(at, lanes):
        copies = []
        for s in range(feeds - 1, 0, -1):
            peer = me ^ s
            copies.append(
                pltpu.make_async_remote_copy(
                    src_ref=send.at[0, pl.ds(0, EARLY), peer, :, at, lanes],
                    dst_ref=recv.at[pl.ds(0, EARLY), me, :, at, lanes],
                    send_sem=send_sem.at[0, s],
                    recv_sem=recv_sem.at[0, s],
                    device_id=(peer, place),
                    device_id_type=MESH,
                )
            )
        mine = pltpu.make_async_copy(
            send.at[0, pl.ds(0, EARLY), me, :, at, lanes],
            recv.at[pl.ds(0, EARLY), me, :, at, lanes],
            self_sem.at[0],
        )
        return copies, mine

    def unit_copies(k, u):
        slot = lax.rem(k, 2)
        g = k * UNITS + u
        copies = []
        for s in range(feeds - 1, 0, -1):
            peer = me ^ s
            copies.append(
                pltpu.make_async_remote_copy(
                    src_ref=send.at[slot, u, peer],
                    dst_ref=recv.at[g, me],
                    send_sem=send_sem.at[g, s],
                    recv_sem=recv_sem.at[g, s],
                    device_id=(peer, place),
                    device_id_type=MESH,
                )
            )
        mine = pltpu.make_async_copy(send.at[slot, u, me], recv.at[g, me], self_sem.at[g])
        return copies, mine

    all_rows, all_lanes = pl.ds(0, inputs), pl.ds(0, 2 * frames)
    last_unit = unit_count - 1

    def last_copies(j):
        copies = []
        channel = place ^ j
        for s in range(feeds - 1, 0, -1):
            peer = me ^ s
            copies.append(
                pltpu.make_async_remote_copy(
                    src_ref=send.at[(chunks - 1) % 2, UNITS - 1, peer, channel],
                    dst_ref=recv.at[last_unit, me, channel],
                    send_sem=last_send_sem.at[j, s],
                    recv_sem=last_recv_sem.at[j, s],
                    device_id=(peer, place),
                    device_id_type=MESH,
                )
            )
        return copies

    def send_units(k, first):
        def one(u, unused):
            copies, mine = unit_copies(k, u)
            mine.start()

            @pl.when(k * UNITS + u < last_unit)
            def _():
                for copy in copies:
                    copy.start()

            @pl.when(k * UNITS + u == last_unit)
            def _():
                for j in ORDER:
                    for copy in last_copies(j):
                        copy.start()

            return unused

        lax.fori_loop(first, UNITS, one, 0)

    def sent(k):
        @pl.when(k == 0)
        def _():
            copies, _ = head_copies(all_rows, all_lanes)
            for copy in copies:
                copy.wait_send()

        def one(u, unused):
            g = k * UNITS + u

            @pl.when(jnp.logical_and(g >= EARLY, g < last_unit))
            def _():
                copies, _ = unit_copies(k, u)
                for copy in copies:
                    copy.wait_send()

            @pl.when(g == last_unit)
            def _():
                for j in ORDER:
                    for copy in last_copies(j):
                        copy.wait_send()

            return unused

        lax.fori_loop(0, UNITS, one, 0)

    def arrived(g):
        @pl.when(g == 0)
        def _():
            copies, mine = head_copies(all_rows, all_lanes)
            for copy in copies:
                copy.wait_recv()
            mine.wait()

        @pl.when(g >= EARLY)
        def _():
            copies, mine = unit_copies(g // UNITS, lax.rem(g, UNITS))
            mine.wait()

            @pl.when(g < last_unit)
            def _():
                for copy in copies:
                    copy.wait_recv()

    row = lax.broadcasted_iota(jnp.int32, (total, total), 0)
    column = lax.broadcasted_iota(jnp.int32, (total, total), 1)
    dims = (((1,), (1,)), ((), ()))

    middle = jnp.logical_and(place > 0, place < times - 1)

    def zcopy(g, s):
        return pltpu.make_async_remote_copy(
            src_ref=zsend.at[lax.rem(g, RING), s - 1],
            dst_ref=zrecv.at[g, s - 1],
            send_sem=zsend_sem.at[g, s],
            recv_sem=zrecv_sem.at[g, s],
            device_id=(me, place ^ s),
            device_id_type=MESH,
        )

    def relay_copy(g):
        return pltpu.make_async_remote_copy(
            src_ref=zsend.at[lax.rem(g, RING), 2],
            dst_ref=relay.at[g],
            send_sem=zsend_sem.at[g, 3],
            recv_sem=relay_sem.at[g],
            device_id=(me, place ^ 1),
            device_id_type=MESH,
        )

    def out_copy(g):
        slot = lax.rem(g, RING)
        return pltpu.make_async_copy(own.at[slot], out_ref.at[g], out_sem.at[slot])

    def gram(g):
        arrived(g)
        slot = lax.rem(g, RING)

        @pl.when(g >= RING)
        def _():
            for s in range(1, times):
                zcopy(g - RING, s).wait_send()
            out_copy(g - RING).wait()

        for s in ORDER:
            @pl.when(g == last_unit)
            def _():
                for copy in last_copies(s):
                    copy.wait_recv()

            slab = recv[g, :, place ^ s].reshape(total, 2 * frames)
            columns = [slab[:, j * width : (j + 1) * width] for j in range(2 * parts)]
            swapped = [-columns[j - 1] if j % 2 else columns[j + 1] for j in range(2 * parts)]
            swapped = jnp.concatenate(swapped, axis=1)
            real = lax.dot_general(slab, slab, dims, preferred_element_type=jnp.float32)
            imag = lax.dot_general(swapped, slab, dims, preferred_element_type=jnp.float32)
            packed = jnp.where(row <= column, real, imag)
            if s == 0:
                own[slot] = packed
            elif s == 1:
                code(packed, slot, s)
                zcopy(g, s).start()
            elif s == 3:
                code(packed, slot, s)
                passed_on = jnp.logical_and(jnp.logical_not(middle), g < relayed)

                @pl.when(passed_on)
                def _():
                    relay_copy(g).start()

                @pl.when(jnp.logical_not(passed_on))
                def _():
                    zcopy(g, s).start()
            else:
                held_back = jnp.logical_and(middle, g < relayed)

                @pl.when(held_back)
                def _():
                    far[lax.rem(g, 2)] = packed

                @pl.when(jnp.logical_not(held_back))
                def _():
                    code(packed, slot, s)
                    zcopy(g, s).start()

    def code(packed, slot, s):
        diagonal = jnp.where(row == column, packed, 0.0)
        powers = [
            jnp.ceil(0.5 * jnp.log2(jnp.maximum(jnp.sum(diagonal, axis=a, keepdims=True), 1e-30)))
            for a in range(2)
        ]
        scaled = packed * (LEVELS * jnp.exp2(-powers[0])) * jnp.exp2(-powers[1])
        zsend[slot, s - 1, :total] = jnp.round(scaled).astype(jnp.int32).astype(jnp.int16)
        note = jnp.broadcast_to(powers[0], (NOTE_ROWS, total))
        zsend[slot, s - 1, total:] = note.astype(jnp.int32).astype(jnp.int16)

    def decoded(value, note):
        across = jnp.exp2(note.astype(jnp.int32).astype(jnp.float32))[:1]
        down = jnp.sum(jnp.where(row == column, across, 0.0), axis=1, keepdims=True)
        return value.astype(jnp.int32).astype(jnp.float32) * across * (down * (1.0 / LEVELS))

    def pass_on(g):
        @pl.when(jnp.logical_and(middle, g < relayed))
        def _():
            relay_copy(g).wait_recv()
            both = far[lax.rem(g, 2)] + decoded(relay[g, :total], relay[g, total:])
            code(both, lax.rem(g, RING), 2)
            zcopy(g, 2).start()

    def finish(g):
        slot = lax.rem(g, RING)
        for s in (1, 2):
            zcopy(g, s).wait_recv()
            own[slot] += decoded(zrecv[g, s - 1, :total], zrecv[g, s - 1, total:])

        @pl.when(jnp.logical_or(middle, g >= relayed))
        def _():
            zcopy(g, 3).wait_recv()
            own[slot] += decoded(zrecv[g, 2, :total], zrecv[g, 2, total:])

        out_copy(g).start()

    for n in range(STAGES - 1):
        block_start(jnp.int32(n))

    def head(j, unused):
        h, part = quarter(j)
        filter_part(j)

        transform(0, h, part)

        @pl.when(j == 0)
        def _():
            pl.semaphore_wait(barrier, feeds + times - 2)

            @pl.when(place < times - 1)
            def _():
                history_copy().start()

        copies, mine = head_copies(
            half_rows(h), pl.ds(pl.multiple_of(part * 2 * width, 2 * width), 2 * width)
        )
        for copy in copies:
            copy.start()
        mine.start()
        return unused

    lax.fori_loop(0, halves * parts, head, 0)
    send_units(jnp.int32(0), EARLY)

    lag = RING - 1

    def units_of(k):
        def one(u, unused):
            g = k * UNITS + u

            @pl.when(g >= 1)
            def _():
                pass_on(g - 1)

            @pl.when(g >= lag)
            def _():
                finish(g - lag)

            gram(g)

            return unused

        lax.fori_loop(0, UNITS, one, 0)

    def main(k, unused):
        @pl.when(k < chunks)
        def _():
            @pl.when(k >= 2)
            def _():
                sent(k - 2)

            def some(j, unused):
                h, part = quarter(j)
                transform(k, h, part)
                return unused

            lax.fori_loop(0, halves * parts, some, 0)
            send_units(k, 0)

        units_of(k - 1)
        return unused

    lax.fori_loop(1, chunks + 1, main, 0)

    def last(j, unused):
        finish(unit_count - lag + j)
        return unused

    lax.fori_loop(0, lag, last, 0)

    for k in range(max(chunks - 2, 0), chunks):
        sent(k)

    def drain(j, unused):
        g = unit_count - RING + j
        for s in range(1, times):
            zcopy(g, s).wait_send()
        out_copy(g).wait()
        return unused

    lax.fori_loop(0, RING, drain, 0)

    @pl.when(place < times - 1)
    def _():
        history_copy().wait_send()


def whole_call(voltages, filter_taps, table, slopes, delays):
    feeds, times = lax.axis_size("feed"), lax.axis_size("tm")
    inputs, sample_count = voltages.shape
    tap_count, fft_length = filter_taps.shape
    frames = sample_count // fft_length
    chunks, rows = table.shape[0], table.shape[1] // 2
    units = chunks * UNITS
    total = feeds * inputs
    kept = tap_count - 1
    vmem = pl.BlockSpec(memory_space=pltpu.VMEM)
    return pl.pallas_call(
        whole_kernel,
        out_shape=jax.ShapeDtypeStruct((units, total, total), jnp.float32),
        in_specs=[pl.BlockSpec(memory_space=pl.ANY), vmem, vmem, vmem, vmem],
        out_specs=pl.BlockSpec(memory_space=pl.ANY),
        scratch_shapes=[
            pltpu.VMEM((STAGES, HALF, (GROUP + kept) * fft_length), jnp.bfloat16),
            pltpu.VMEM((inputs, kept * fft_length), jnp.bfloat16),
            pltpu.VMEM((inputs, frames, fft_length), jnp.bfloat16),
            pltpu.VMEM((2, rows * PITCH, 128), jnp.float32),
            pltpu.VMEM((2, UNITS, feeds, times, inputs, 2 * frames), jnp.bfloat16),
            pltpu.VMEM((units, feeds, times, inputs, 2 * frames), jnp.bfloat16),
            pltpu.VMEM((RING, total, total), jnp.float32),
            pltpu.VMEM((2, total, total), jnp.float32),
            pltpu.VMEM((RING, times - 1, total + NOTE_ROWS, total), jnp.int16),
            pltpu.VMEM((units, times - 1, total + NOTE_ROWS, total), jnp.int16),
            pltpu.VMEM((units - DIRECT, total + NOTE_ROWS, total), jnp.int16),
            pltpu.SemaphoreType.DMA((STAGES,)),
            pltpu.SemaphoreType.DMA((2,)),
            pltpu.SemaphoreType.DMA((units, feeds)),
            pltpu.SemaphoreType.DMA((units, feeds)),
            pltpu.SemaphoreType.DMA((units,)),
            pltpu.SemaphoreType.DMA((units, times)),
            pltpu.SemaphoreType.DMA((units, times)),
            pltpu.SemaphoreType.DMA((units - DIRECT,)),
            pltpu.SemaphoreType.DMA((RING,)),
            pltpu.SemaphoreType.DMA((times, feeds)),
            pltpu.SemaphoreType.DMA((times, feeds)),
        ],
        compiler_params=pltpu.CompilerParams(
            vmem_limit_bytes=VMEM_WHOLE, collective_id=0, has_side_effects=True
        ),
        cost_estimate=pl.CostEstimate(
            flops=8 * inputs * sample_count * 512,
            bytes_accessed=4 * inputs * sample_count,
            transcendentals=0,
        ),
    )(voltages, filter_taps, table, slopes, delays)


def whole_fits(voltages, filter_taps, channel_flags, feeds, times):
    inputs, frames = voltages.shape[0], voltages.shape[1] // filter_taps.shape[1]
    kept = channel_flags.shape[0] // times
    rows = UNITS * feeds * times
    if times != 4 or inputs % HALF or feeds & (feeds - 1) or kept % UNITS or frames % 128:
        return False
    if kept < 2 * UNITS or frames < 2 * GROUP:
        return False
    spectra = 2 * inputs * 2 * frames
    total = feeds * inputs
    held = 2 * inputs * voltages.shape[1]
    held += spectra * (2 * rows + kept * feeds * times) + 1024 * rows * PITCH
    held += 2 * STAGES * HALF * (GROUP + 3) * filter_taps.shape[1]
    held += 2 * ((RING + kept) * (times - 1) + kept - DIRECT) * (total + NOTE_ROWS) * total
    held += 4 * (RING + 2) * total * total
    return held < VMEM_WHOLE - 3 * 1000 * 1000


def on_device_whole(voltages, filter_taps, delays, channel_flags):
    inputs = voltages.shape[0]
    fft_length = filter_taps.shape[1]
    feeds, times = lax.axis_size("feed"), lax.axis_size("tm")
    frame_total = voltages.shape[1] // fft_length * times
    owned = channel_flags.shape[0]
    kept = owned // times
    chunks = kept // UNITS
    order = np.arange(feeds * owned).reshape(feeds, times, chunks, UNITS)
    order = order.transpose(2, 3, 0, 1).reshape(chunks, -1)
    table = jnp.asarray(np.stack([table_rows(order[k], fft_length) for k in range(chunks)]))
    slopes = np.float32(2.0 * math.pi / fft_length) * order.astype(np.float32)
    slopes = jnp.asarray(slopes[:, None, :])
    vis = whole_call(voltages, filter_taps, table, slopes, delays.reshape(1, inputs))
    flags = lax.dynamic_slice_in_dim(channel_flags, lax.axis_index("tm") * kept, kept, 0)
    return vis * (flags.astype(jnp.float32) * (1.0 / frame_total))[:, None, None]


def on_device(voltages, filter_taps, delays, channel_flags):
    feeds, times = lax.axis_size("feed"), lax.axis_size("tm")
    if whole_fits(voltages, filter_taps, channel_flags, feeds, times):
        return on_device_whole(voltages, filter_taps, delays, channel_flags)
    return on_device_steps(voltages, filter_taps, delays, channel_flags)


def solution(mesh):
    in_specs = (P("feed", "tm"), P(), P("feed"), P("feed"))
    out_specs = P(("feed", "tm"), None, None)
    return jax.shard_map(
        on_device, mesh=mesh, in_specs=in_specs, out_specs=out_specs, check_vma=False
    )
```

```python
import functools
import math

import jax
import jax.numpy as jnp
import numpy as np
from jax import lax
from jax.experimental import pallas as pl
from jax.experimental.pallas import tpu as pltpu
from jax.sharding import PartitionSpec as P

VMEM_LIMIT = 56 * 1024 * 1024
SEND_PEAK = 16384.0
EXTRA_ROWS = 8


def passed_along(block, axis, distance):
    devices = range(lax.axis_size(axis))
    route = [(i - distance, i) for i in devices if i - distance in devices]
    return lax.ppermute(block, axis, route)


def table_rows(channels, fft_length):
    samples = np.arange(fft_length, dtype=np.int64)
    product = channels[:, None].astype(np.int64) * samples[None, :] % fft_length
    angles = product.astype(np.float32) * np.float32(2.0 * math.pi / fft_length)
    rows = np.concatenate([np.cos(angles), -np.sin(angles)], axis=0)
    return rows.astype(jnp.bfloat16)


def dft_kernel(table_ref, cos_ref, sin_ref, filtered_ref, out_ref, *turned):
    inputs, frames = filtered_ref.shape[0], filtered_ref.shape[1]
    rows = table_ref.shape[0] // 2
    width = 128
    for i in range(inputs):
        raw = lax.dot_general(
            table_ref[...], filtered_ref[i], (((1,), (1,)), ((), ())),
            preferred_element_type=jnp.float32,
        )
        real, imag = raw[:rows], raw[rows:]
        cosine = cos_ref[0, :, i : i + 1]
        sine = sin_ref[0, :, i : i + 1]
        both = (real * cosine + imag * sine, imag * cosine - real * sine)
        for q in range(2):
            for piece in range(frames // width):
                turned[q * (frames // width) + piece][pl.ds(i, rows, stride=inputs), :] = both[q][
                    :, piece * width : (piece + 1) * width
                ]
    for piece, ref in enumerate(turned):
        value = ref[...].reshape(rows, inputs, width).astype(jnp.bfloat16)
        out_ref[:, :, piece * width : (piece + 1) * width] = value


def dft_call(table, cosine, sine, filtered):
    blocks, rows, inputs = cosine.shape
    inputs_here, frames, fft_length = filtered.shape
    out_shape = jax.ShapeDtypeStruct((rows, inputs_here, 2 * frames), jnp.bfloat16)
    return pl.pallas_call(
        dft_kernel,
        out_shape=out_shape,
        grid=(blocks,),
        in_specs=[
            pl.BlockSpec((2 * rows, fft_length), lambda b: (0, 0)),
            pl.BlockSpec((1, rows, inputs), lambda b: (b, 0, 0)),
            pl.BlockSpec((1, rows, inputs), lambda b: (b, 0, 0)),
            pl.BlockSpec((inputs, frames, fft_length), lambda b: (b, 0, 0)),
        ],
        out_specs=pl.BlockSpec((rows, inputs, 2 * frames), lambda b: (0, b, 0)),
        scratch_shapes=[pltpu.VMEM((rows * inputs, 128), jnp.float32)] * (2 * frames // 128),
        compiler_params=pltpu.CompilerParams(vmem_limit_bytes=VMEM_LIMIT),
        cost_estimate=pl.CostEstimate(
            flops=10 * 4 * rows * inputs_here * frames * fft_length,
            bytes_accessed=2 * inputs_here * frames * (fft_length + 2 * rows),
            transcendentals=0,
        ),
    )(table, cosine, sine, filtered)


def gram_kernel(spectra_ref, vis_ref):
    sources, channels, inputs_here, columns = spectra_ref.shape
    total = sources * inputs_here
    half = columns // 2
    row = lax.broadcasted_iota(jnp.int32, (total, total), 0)
    column = lax.broadcasted_iota(jnp.int32, (total, total), 1)
    dims = (((1,), (1,)), ((), ()))
    for c in range(channels):
        slab = spectra_ref[:, c]
        if inputs_here % 16:
            slab = slab.astype(jnp.float32).reshape(total, columns).astype(jnp.bfloat16)
        else:
            slab = slab.reshape(total, columns)
        swapped = jnp.concatenate([slab[:, half:], -slab[:, :half]], axis=1)
        real = lax.dot_general(slab, slab, dims, preferred_element_type=jnp.float32)
        imag = lax.dot_general(swapped, slab, dims, preferred_element_type=jnp.float32)
        packed = jnp.where(row <= column, real, imag)
        peak = jnp.max(jnp.where(row == column, real, 0.0), axis=(0, 1), keepdims=True)
        peak = jnp.maximum(peak, 1e-30)
        power = jnp.ceil(jnp.log2(peak))
        vis_ref[c, :total] = packed * (SEND_PEAK * jnp.exp2(-power))
        vis_ref[c, total:] = jnp.broadcast_to(power, (EXTRA_ROWS, total))


def gram_call(spectra):
    sources, channels, inputs_here, columns = spectra.shape
    total = sources * inputs_here
    step = 2 if channels % 2 == 0 else 1
    return pl.pallas_call(
        gram_kernel,
        out_shape=jax.ShapeDtypeStruct((channels, total + EXTRA_ROWS, total), jnp.float32),
        grid=(channels // step,),
        in_specs=[pl.BlockSpec((sources, step, inputs_here, columns), lambda b: (0, b, 0, 0))],
        out_specs=pl.BlockSpec((step, total + EXTRA_ROWS, total), lambda b: (b, 0, 0)),
        compiler_params=pltpu.CompilerParams(vmem_limit_bytes=VMEM_LIMIT),
        cost_estimate=pl.CostEstimate(
            flops=40 * 4 * channels * total * total * columns,
            bytes_accessed=2 * channels * total * (columns + 2 * total),
            transcendentals=0,
        ),
    )(spectra)


def filter_kernel(history_ref, taps_ref, block_ref, out_ref, carry, turned):
    tap_count, fft_length = taps_ref.shape
    inputs, group = out_ref.shape[0], out_ref.shape[1]
    kept = tap_count - 1

    @pl.when(pl.program_id(0) == 0)
    def _():
        carry[...] = history_ref[...]

    def piece(p, unused):
        lanes = pl.multiple_of(p * 128, 128)
        taps = [taps_ref[t : t + 1, pl.ds(lanes, 128)] for t in range(tap_count)]
        frames = [
            carry[:, pl.ds(pl.multiple_of(h * fft_length + lanes, 128), 128)].astype(jnp.float32)
            for h in range(kept)
        ]
        for m in range(group):
            start = pl.multiple_of(m * fft_length + lanes, 128)
            frames.append(block_ref[:, pl.ds(start, 128)].astype(jnp.float32))
            value = taps[0] * frames[-1]
            for t in range(1, tap_count):
                value = value + taps[t] * frames[-1 - t]
            turned[pl.ds(m, inputs, stride=group), :] = value
        result = turned[...].reshape(inputs, group, 128).astype(jnp.bfloat16)
        out_ref[:, :, pl.ds(lanes, 128)] = result
        return unused

    lax.fori_loop(0, fft_length // 128, piece, 0)
    carry[...] = block_ref[:, (group - kept) * fft_length :]


def filter_frames(voltages, filter_taps):
    inputs_here, sample_count = voltages.shape
    tap_count, fft_length = filter_taps.shape
    frames = sample_count // fft_length
    kept = (tap_count - 1) * fft_length
    group = 16
    history = passed_along(voltages[:, sample_count - kept :], "tm", 1)
    return pl.pallas_call(
        filter_kernel,
        out_shape=jax.ShapeDtypeStruct((inputs_here, frames, fft_length), jnp.bfloat16),
        grid=(frames // group,),
        in_specs=[
            pl.BlockSpec((inputs_here, kept), lambda b: (0, 0)),
            pl.BlockSpec((tap_count, fft_length), lambda b: (0, 0)),
            pl.BlockSpec((inputs_here, group * fft_length), lambda b: (0, b)),
        ],
        out_specs=pl.BlockSpec((inputs_here, group, fft_length), lambda b: (0, b, 0)),
        scratch_shapes=[
            pltpu.VMEM((inputs_here, kept), jnp.bfloat16),
            pltpu.VMEM((inputs_here * group, 128), jnp.float32),
        ],
        compiler_params=pltpu.CompilerParams(vmem_limit_bytes=VMEM_LIMIT),
        cost_estimate=pl.CostEstimate(
            flops=8 * inputs_here * sample_count,
            bytes_accessed=4 * inputs_here * sample_count,
            transcendentals=0,
        ),
    )(history, filter_taps, voltages)


def on_device_steps(voltages, filter_taps, delays, channel_flags):
    inputs_here = voltages.shape[0]
    fft_length = filter_taps.shape[1]
    feeds, times = lax.axis_size("feed"), lax.axis_size("tm")
    filtered = filter_frames(voltages, filter_taps)
    frame_total = filtered.shape[1] * times
    owned = channel_flags.shape[0]
    kept = owned // times
    chunks = 4 if kept % 4 == 0 else 1
    width = kept // chunks
    block = 16 if inputs_here % 16 == 0 else inputs_here

    local_flags = lax.dynamic_slice_in_dim(
        channel_flags, lax.axis_index("tm") * kept, kept, 0
    ).astype(jnp.float32)
    flag_parts = (local_flags * (1.0 / (SEND_PEAK * frame_total))).reshape(chunks, width)
    scale = 1.0 / math.sqrt(fft_length)
    order = np.arange(feeds * owned).reshape(feeds, times, chunks, width)
    place = lax.axis_index("tm")

    def summed(vis, flags):
        total = 0.0
        for shift in range(times):
            target = lax.rem(place + shift, times)
            part = lax.dynamic_index_in_dim(vis, target, 0, keepdims=False)
            if shift:
                route = [(i, (i + shift) % times) for i in range(times)]
                part = lax.ppermute(part, "tm", route)
            part = part.astype(jnp.float32)
            count = part.shape[2]
            total = total + part[:, :count] * jnp.exp2(part[:, count:, :1][:, :1])
        return total * flags[:, None, None]

    results = []
    sent = []
    for k in range(chunks):
        channels = order[:, :, k].reshape(-1)
        table = jnp.asarray(table_rows(channels, fft_length))
        angles = 2.0 * math.pi / fft_length * jnp.asarray(channels, jnp.float32)[None, :, None]
        angles = angles * delays.reshape(-1, 1, block)
        if k >= 2:
            filtered, sent[k - 2] = lax.optimization_barrier((filtered, sent[k - 2]))
            results.append(summed(sent[k - 2], flag_parts[k - 2]))
        spectra = dft_call(table, jnp.cos(angles) * scale, jnp.sin(angles) * scale, filtered)
        spectra = spectra.reshape(feeds, times * width, inputs_here, spectra.shape[2])
        if k >= 3:
            spectra, results[k - 3] = lax.optimization_barrier((spectra, results[k - 3]))
        turned = lax.all_to_all(spectra, "feed", split_axis=0, concat_axis=0, tiled=True)
        if k >= 2:
            turned, results[k - 2] = lax.optimization_barrier((turned, results[k - 2]))
        vis = gram_call(turned).astype(jnp.float16)
        sent.append(vis.reshape(times, width, vis.shape[1], vis.shape[2]))
    for k in range(len(results), chunks):
        results.append(summed(sent[k], flag_parts[k]))
    return jnp.concatenate(results, axis=0)


VMEM_WHOLE = 64 * 1000 * 1000
MESH = pl.DeviceIdType.MESH
HALF = 16
GROUP = 16
UNITS = 4
EARLY = 3
LEVELS = 32760.0
NOTE_ROWS = 16
RING = 3
DIRECT = 1
ORDER = (3, 2, 1, 0)
STAGES = 4
PITCH = GROUP + 1


def whole_kernel(
    volt_ref, taps_ref, table_ref, slope_ref, delay_ref, out_ref,
    stage, history, filtered, turned, send, recv, own, far, zsend, zrecv, relay,
    stage_sem, history_sems, send_sem, recv_sem, self_sem, zsend_sem, zrecv_sem, relay_sem, out_sem,
    last_send_sem, last_recv_sem,
):
    feeds, times = lax.axis_size("feed"), lax.axis_size("tm")
    me, place = lax.axis_index("feed"), lax.axis_index("tm")
    inputs, sample_count = volt_ref.shape
    tap_count, fft_length = taps_ref.shape
    frames = sample_count // fft_length
    kept = tap_count - 1
    halves = inputs // HALF
    chunks = table_ref.shape[0]
    rows = table_ref.shape[1] // 2
    unit_count = chunks * UNITS
    peers = [s for bit in (1, 0) for s in range(feeds - 1, 0, -1) if (s ^ s // 2) & 1 == bit]
    relayed = relay.shape[0]
    total = feeds * inputs
    width = 128
    parts = frames // width
    part_groups = width // GROUP

    barrier = pltpu.get_barrier_semaphore()
    for s in range(1, feeds):
        pl.semaphore_signal(barrier, inc=1, device_id=(me ^ s, place), device_id_type=MESH)
    for s in range(1, times):
        other = lax.rem(place + s, times)
        pl.semaphore_signal(barrier, inc=1, device_id=(me, other), device_id_type=MESH)
    def history_copy():
        return pltpu.make_async_remote_copy(
            src_ref=volt_ref.at[:, pl.ds(sample_count - kept * fft_length, kept * fft_length)],
            dst_ref=history,
            send_sem=history_sems.at[0],
            recv_sem=history_sems.at[1],
            device_id=(me, place + 1),
            device_id_type=MESH,
        )

    head_steps = halves * parts * part_groups

    def quarter(j):
        return j // parts, parts - 1 - lax.rem(j, parts)

    def block_copies(n):
        h, part = quarter(n // part_groups)
        g = part * part_groups + lax.rem(lax.rem(n, part_groups) + 1, part_groups)
        slot = lax.rem(n, STAGES)
        at = half_rows(h)
        first = pl.multiple_of(jnp.maximum(g * GROUP - kept, 0) * fft_length, 128)
        later = pltpu.make_async_copy(
            volt_ref.at[at, pl.ds(first, (GROUP + kept) * fft_length)],
            stage.at[slot],
            stage_sem.at[slot],
        )
        start = pltpu.make_async_copy(
            volt_ref.at[at, pl.ds(0, GROUP * fft_length)],
            stage.at[slot, :, pl.ds(kept * fft_length, GROUP * fft_length)],
            stage_sem.at[slot],
        )
        return g, slot, later, start

    def block_start(n):
        g, _, later, start = block_copies(n)

        @pl.when(g > 0)
        def _():
            later.start()

        @pl.when(g == 0)
        def _():
            start.start()

    def filter_part(j):
        h, _ = quarter(j)

        def step_body(step, unused):
            n = j * part_groups + step

            @pl.when(n + STAGES - 1 < head_steps)
            def _():
                block_start(n + STAGES - 1)

            g, slot, later, start = block_copies(n)

            @pl.when(g > 0)
            def _():
                later.wait()

            @pl.when(g == 0)
            def _():
                start.wait()

                @pl.when(place == 0)
                def _():
                    stage[slot, :, : kept * fft_length] = jnp.zeros(
                        (HALF, kept * fft_length), jnp.bfloat16
                    )

                @pl.when(place > 0)
                def _():
                    @pl.when(h == 0)
                    def _():
                        history_copy().wait_recv()

                    stage[slot, :, : kept * fft_length] = history[half_rows(h), :]

            of = pl.ds(pl.multiple_of(g * GROUP, GROUP), GROUP)
            for lane in range(0, fft_length, width):
                taps = [taps_ref[t : t + 1, lane : lane + width] for t in range(tap_count)]

                def frame(j):
                    column = j * fft_length + lane
                    return stage[slot, :, column : column + width].astype(jnp.float32)

                window = [frame(j) for j in range(kept)]
                for m in range(GROUP):
                    window.append(frame(m + kept))
                    value = taps[0] * window[-1]
                    for t in range(1, tap_count):
                        value = value + taps[t] * window[-1 - t]
                    turned[0, pl.ds(m, HALF, stride=PITCH), :] = value
                for i in range(HALF):
                    rows_here = turned[0, i * PITCH : i * PITCH + GROUP]
                    filtered[h * HALF + i, of, lane : lane + width] = rows_here.astype(jnp.bfloat16)
            return unused

        lax.fori_loop(0, part_groups, step_body, 0)

    def transform(k, h, part):
        slot = lax.rem(k, 2)
        span = pl.ds(pl.multiple_of(part * width, width), width)
        block = filtered[half_rows(h), span].reshape(HALF * width, fft_length)
        raw = lax.dot_general(
            block, table_ref[k], (((1,), (1,)), ((), ())), preferred_element_type=jnp.float32
        )
        across = lax.broadcasted_iota(jnp.int32, (HALF, inputs), 1) - h * HALF
        mine = lax.broadcasted_iota(jnp.int32, (HALF, inputs), 0) == across
        delay = jnp.sum(jnp.where(mine, delay_ref[...], 0.0), axis=1, keepdims=True)
        angles = slope_ref[k] * delay
        scale = 1.0 / math.sqrt(fft_length)
        cosines, sines = jnp.cos(angles) * scale, jnp.sin(angles) * scale
        for i in range(HALF):
            here = raw[i * width : (i + 1) * width]
            real, imag = here[:, :rows], here[:, rows:]
            cosine = cosines[i : i + 1]
            sine = sines[i : i + 1]
            both = (real * cosine + imag * sine, imag * cosine - real * sine)
            for q in range(2):
                turned[q, pl.ds(i, rows, stride=PITCH), :] = jnp.transpose(both[q])
        for q in range(2):
            lanes = pl.ds(pl.multiple_of((2 * part + q) * width, width), width)
            for r in range(rows):
                u, f, t = r // (feeds * times), r // times % feeds, r % times
                value = turned[q, r * PITCH : r * PITCH + HALF].astype(jnp.bfloat16)
                send[slot, u, f, t, half_rows(h), lanes] = value

    def half_rows(h):
        return pl.ds(pl.multiple_of(h * HALF, HALF), HALF)

    def head_copies(at, lanes):
        copies = []
        for s in peers:
            peer = me ^ s
            copies.append(
                pltpu.make_async_remote_copy(
                    src_ref=send.at[0, pl.ds(0, EARLY), peer, :, at, lanes],
                    dst_ref=recv.at[pl.ds(0, EARLY), me, :, at, lanes],
                    send_sem=send_sem.at[0, s],
                    recv_sem=recv_sem.at[0, s],
                    device_id=(peer, place),
                    device_id_type=MESH,
                )
            )
        mine = pltpu.make_async_copy(
            send.at[0, pl.ds(0, EARLY), me, :, at, lanes],
            recv.at[pl.ds(0, EARLY), me, :, at, lanes],
            self_sem.at[0],
        )
        return copies, mine

    def unit_copies(k, u):
        slot = lax.rem(k, 2)
        g = k * UNITS + u
        copies = []
        for s in peers:
            peer = me ^ s
            copies.append(
                pltpu.make_async_remote_copy(
                    src_ref=send.at[slot, u, peer],
                    dst_ref=recv.at[g, me],
                    send_sem=send_sem.at[g, s],
                    recv_sem=recv_sem.at[g, s],
                    device_id=(peer, place),
                    device_id_type=MESH,
                )
            )
        mine = pltpu.make_async_copy(send.at[slot, u, me], recv.at[g, me], self_sem.at[g])
        return copies, mine

    all_rows, all_lanes = pl.ds(0, inputs), pl.ds(0, 2 * frames)
    last_unit = unit_count - 1

    def last_copies(j):
        copies = []
        channel = place ^ j
        for s in peers:
            peer = me ^ s
            copies.append(
                pltpu.make_async_remote_copy(
                    src_ref=send.at[(chunks - 1) % 2, UNITS - 1, peer, channel],
                    dst_ref=recv.at[last_unit, me, channel],
                    send_sem=last_send_sem.at[j, s],
                    recv_sem=last_recv_sem.at[j, s],
                    device_id=(peer, place),
                    device_id_type=MESH,
                )
            )
        return copies

    def send_units(k, first):
        def one(u, unused):
            copies, mine = unit_copies(k, u)
            mine.start()

            @pl.when(k * UNITS + u < last_unit)
            def _():
                for copy in copies:
                    copy.start()

            @pl.when(k * UNITS + u == last_unit)
            def _():
                for j in ORDER:
                    for copy in last_copies(j):
                        copy.start()

            return unused

        lax.fori_loop(first, UNITS, one, 0)

    def sent(k):
        @pl.when(k == 0)
        def _():
            copies, _ = head_copies(all_rows, all_lanes)
            for copy in copies:
                copy.wait_send()

        def one(u, unused):
            g = k * UNITS + u

            @pl.when(jnp.logical_and(g >= EARLY, g < last_unit))
            def _():
                copies, _ = unit_copies(k, u)
                for copy in copies:
                    copy.wait_send()

            @pl.when(g == last_unit)
            def _():
                for j in ORDER:
                    for copy in last_copies(j):
                        copy.wait_send()

            return unused

        lax.fori_loop(0, UNITS, one, 0)

    def arrived(g):
        @pl.when(g == 0)
        def _():
            copies, mine = head_copies(all_rows, all_lanes)
            for copy in copies:
                copy.wait_recv()
            mine.wait()

        @pl.when(g >= EARLY)
        def _():
            copies, mine = unit_copies(g // UNITS, lax.rem(g, UNITS))
            mine.wait()

            @pl.when(g < last_unit)
            def _():
                for copy in copies:
                    copy.wait_recv()

    row = lax.broadcasted_iota(jnp.int32, (total, total), 0)
    column = lax.broadcasted_iota(jnp.int32, (total, total), 1)
    dims = (((1,), (1,)), ((), ()))

    middle = jnp.logical_and(place > 0, place < times - 1)

    def zcopy(g, s):
        return pltpu.make_async_remote_copy(
            src_ref=zsend.at[lax.rem(g, RING), s - 1],
            dst_ref=zrecv.at[g, s - 1],
            send_sem=zsend_sem.at[g, s],
            recv_sem=zrecv_sem.at[g, s],
            device_id=(me, place ^ s),
            device_id_type=MESH,
        )

    def relay_copy(g):
        return pltpu.make_async_remote_copy(
            src_ref=zsend.at[lax.rem(g, RING), 2],
            dst_ref=relay.at[g],
            send_sem=zsend_sem.at[g, 3],
            recv_sem=relay_sem.at[g],
            device_id=(me, place ^ 1),
            device_id_type=MESH,
        )

    def out_copy(g):
        slot = lax.rem(g, RING)
        return pltpu.make_async_copy(own.at[slot], out_ref.at[g], out_sem.at[slot])

    def gram(g):
        arrived(g)
        slot = lax.rem(g, RING)

        @pl.when(g >= RING)
        def _():
            for s in range(1, times):
                zcopy(g - RING, s).wait_send()
            out_copy(g - RING).wait()

        for s in ORDER:
            @pl.when(g == last_unit)
            def _():
                for copy in last_copies(s):
                    copy.wait_recv()

            slab = recv[g, :, place ^ s].reshape(total, 2 * frames)
            columns = [slab[:, j * width : (j + 1) * width] for j in range(2 * parts)]
            swapped = [-columns[j - 1] if j % 2 else columns[j + 1] for j in range(2 * parts)]
            swapped = jnp.concatenate(swapped, axis=1)
            real = lax.dot_general(slab, slab, dims, preferred_element_type=jnp.float32)
            imag = lax.dot_general(swapped, slab, dims, preferred_element_type=jnp.float32)
            packed = jnp.where(row <= column, real, imag)
            if s == 0:
                own[slot] = packed
            elif s == 1:
                code(packed, slot, s)
                zcopy(g, s).start()
            elif s == 3:
                code(packed, slot, s)
                passed_on = jnp.logical_and(jnp.logical_not(middle), g < relayed)

                @pl.when(passed_on)
                def _():
                    relay_copy(g).start()

                @pl.when(jnp.logical_not(passed_on))
                def _():
                    zcopy(g, s).start()
            else:
                held_back = jnp.logical_and(middle, g < relayed)

                @pl.when(held_back)
                def _():
                    far[lax.rem(g, 2)] = packed

                @pl.when(jnp.logical_not(held_back))
                def _():
                    code(packed, slot, s)
                    zcopy(g, s).start()

    def code(packed, slot, s):
        diagonal = jnp.where(row == column, packed, 0.0)
        powers = [
            jnp.ceil(0.5 * jnp.log2(jnp.maximum(jnp.sum(diagonal, axis=a, keepdims=True), 1e-30)))
            for a in range(2)
        ]
        scaled = packed * (LEVELS * jnp.exp2(-powers[0])) * jnp.exp2(-powers[1])
        zsend[slot, s - 1, :total] = jnp.round(scaled).astype(jnp.int32).astype(jnp.int16)
        note = jnp.broadcast_to(powers[0], (NOTE_ROWS, total))
        zsend[slot, s - 1, total:] = note.astype(jnp.int32).astype(jnp.int16)

    def decoded(value, note):
        across = jnp.exp2(note.astype(jnp.int32).astype(jnp.float32))[:1]
        down = jnp.sum(jnp.where(row == column, across, 0.0), axis=1, keepdims=True)
        return value.astype(jnp.int32).astype(jnp.float32) * across * (down * (1.0 / LEVELS))

    def pass_on(g):
        @pl.when(jnp.logical_and(middle, g < relayed))
        def _():
            relay_copy(g).wait_recv()
            both = far[lax.rem(g, 2)] + decoded(relay[g, :total], relay[g, total:])
            code(both, lax.rem(g, RING), 2)
            zcopy(g, 2).start()

    def finish(g):
        slot = lax.rem(g, RING)
        for s in (1, 2):
            zcopy(g, s).wait_recv()
            own[slot] += decoded(zrecv[g, s - 1, :total], zrecv[g, s - 1, total:])

        @pl.when(jnp.logical_or(middle, g >= relayed))
        def _():
            zcopy(g, 3).wait_recv()
            own[slot] += decoded(zrecv[g, 2, :total], zrecv[g, 2, total:])

        out_copy(g).start()

    for n in range(STAGES - 1):
        block_start(jnp.int32(n))

    def head(j, unused):
        h, part = quarter(j)
        filter_part(j)

        transform(0, h, part)

        @pl.when(j == 0)
        def _():
            pl.semaphore_wait(barrier, feeds + times - 2)

            @pl.when(place < times - 1)
            def _():
                history_copy().start()

        copies, mine = head_copies(
            half_rows(h), pl.ds(pl.multiple_of(part * 2 * width, 2 * width), 2 * width)
        )
        for copy in copies:
            copy.start()
        mine.start()
        return unused

    lax.fori_loop(0, halves * parts, head, 0)
    send_units(jnp.int32(0), EARLY)

    lag = RING - 1

    def units_of(k):
        def one(u, unused):
            g = k * UNITS + u

            @pl.when(g >= 1)
            def _():
                pass_on(g - 1)

            @pl.when(g >= lag)
            def _():
                finish(g - lag)

            gram(g)

            return unused

        lax.fori_loop(0, UNITS, one, 0)

    def main(k, unused):
        @pl.when(k < chunks)
        def _():
            @pl.when(k >= 2)
            def _():
                sent(k - 2)

            def some(j, unused):
                h, part = quarter(j)
                transform(k, h, part)
                return unused

            lax.fori_loop(0, halves * parts, some, 0)
            send_units(k, 0)

        units_of(k - 1)
        return unused

    lax.fori_loop(1, chunks + 1, main, 0)

    def last(j, unused):
        finish(unit_count - lag + j)
        return unused

    lax.fori_loop(0, lag, last, 0)

    for k in range(max(chunks - 2, 0), chunks):
        sent(k)

    def drain(j, unused):
        g = unit_count - RING + j
        for s in range(1, times):
            zcopy(g, s).wait_send()
        out_copy(g).wait()
        return unused

    lax.fori_loop(0, RING, drain, 0)

    @pl.when(place < times - 1)
    def _():
        history_copy().wait_send()


def whole_call(voltages, filter_taps, table, slopes, delays):
    feeds, times = lax.axis_size("feed"), lax.axis_size("tm")
    inputs, sample_count = voltages.shape
    tap_count, fft_length = filter_taps.shape
    frames = sample_count // fft_length
    chunks, rows = table.shape[0], table.shape[1] // 2
    units = chunks * UNITS
    total = feeds * inputs
    kept = tap_count - 1
    vmem = pl.BlockSpec(memory_space=pltpu.VMEM)
    return pl.pallas_call(
        whole_kernel,
        out_shape=jax.ShapeDtypeStruct((units, total, total), jnp.float32),
        in_specs=[pl.BlockSpec(memory_space=pl.ANY), vmem, vmem, vmem, vmem],
        out_specs=pl.BlockSpec(memory_space=pl.ANY),
        scratch_shapes=[
            pltpu.VMEM((STAGES, HALF, (GROUP + kept) * fft_length), jnp.bfloat16),
            pltpu.VMEM((inputs, kept * fft_length), jnp.bfloat16),
            pltpu.VMEM((inputs, frames, fft_length), jnp.bfloat16),
            pltpu.VMEM((2, rows * PITCH, 128), jnp.float32),
            pltpu.VMEM((2, UNITS, feeds, times, inputs, 2 * frames), jnp.bfloat16),
            pltpu.VMEM((units, feeds, times, inputs, 2 * frames), jnp.bfloat16),
            pltpu.VMEM((RING, total, total), jnp.float32),
            pltpu.VMEM((2, total, total), jnp.float32),
            pltpu.VMEM((RING, times - 1, total + NOTE_ROWS, total), jnp.int16),
            pltpu.VMEM((units, times - 1, total + NOTE_ROWS, total), jnp.int16),
            pltpu.VMEM((units - DIRECT, total + NOTE_ROWS, total), jnp.int16),
            pltpu.SemaphoreType.DMA((STAGES,)),
            pltpu.SemaphoreType.DMA((2,)),
            pltpu.SemaphoreType.DMA((units, feeds)),
            pltpu.SemaphoreType.DMA((units, feeds)),
            pltpu.SemaphoreType.DMA((units,)),
            pltpu.SemaphoreType.DMA((units, times)),
            pltpu.SemaphoreType.DMA((units, times)),
            pltpu.SemaphoreType.DMA((units - DIRECT,)),
            pltpu.SemaphoreType.DMA((RING,)),
            pltpu.SemaphoreType.DMA((times, feeds)),
            pltpu.SemaphoreType.DMA((times, feeds)),
        ],
        compiler_params=pltpu.CompilerParams(
            vmem_limit_bytes=VMEM_WHOLE, collective_id=0, has_side_effects=True
        ),
        cost_estimate=pl.CostEstimate(
            flops=8 * inputs * sample_count * 512,
            bytes_accessed=4 * inputs * sample_count,
            transcendentals=0,
        ),
    )(voltages, filter_taps, table, slopes, delays)


def whole_fits(voltages, filter_taps, channel_flags, feeds, times):
    inputs, frames = voltages.shape[0], voltages.shape[1] // filter_taps.shape[1]
    kept = channel_flags.shape[0] // times
    rows = UNITS * feeds * times
    if times != 4 or inputs % HALF or feeds & (feeds - 1) or kept % UNITS or frames % 128:
        return False
    if kept < 2 * UNITS or frames < 2 * GROUP:
        return False
    spectra = 2 * inputs * 2 * frames
    total = feeds * inputs
    held = 2 * inputs * voltages.shape[1]
    held += spectra * (2 * rows + kept * feeds * times) + 1024 * rows * PITCH
    held += 2 * STAGES * HALF * (GROUP + 3) * filter_taps.shape[1]
    held += 2 * ((RING + kept) * (times - 1) + kept - DIRECT) * (total + NOTE_ROWS) * total
    held += 4 * (RING + 2) * total * total
    return held < VMEM_WHOLE - 3 * 1000 * 1000


def on_device_whole(voltages, filter_taps, delays, channel_flags):
    inputs = voltages.shape[0]
    fft_length = filter_taps.shape[1]
    feeds, times = lax.axis_size("feed"), lax.axis_size("tm")
    frame_total = voltages.shape[1] // fft_length * times
    owned = channel_flags.shape[0]
    kept = owned // times
    chunks = kept // UNITS
    order = np.arange(feeds * owned).reshape(feeds, times, chunks, UNITS)
    order = order.transpose(2, 3, 0, 1).reshape(chunks, -1)
    table = jnp.asarray(np.stack([table_rows(order[k], fft_length) for k in range(chunks)]))
    slopes = np.float32(2.0 * math.pi / fft_length) * order.astype(np.float32)
    slopes = jnp.asarray(slopes[:, None, :])
    vis = whole_call(voltages, filter_taps, table, slopes, delays.reshape(1, inputs))
    flags = lax.dynamic_slice_in_dim(channel_flags, lax.axis_index("tm") * kept, kept, 0)
    return vis * (flags.astype(jnp.float32) * (1.0 / frame_total))[:, None, None]


def on_device(voltages, filter_taps, delays, channel_flags):
    feeds, times = lax.axis_size("feed"), lax.axis_size("tm")
    if whole_fits(voltages, filter_taps, channel_flags, feeds, times):
        return on_device_whole(voltages, filter_taps, delays, channel_flags)
    return on_device_steps(voltages, filter_taps, delays, channel_flags)


def solution(mesh):
    in_specs = (P("feed", "tm"), P(), P("feed"), P("feed"))
    out_specs = P(("feed", "tm"), None, None)
    return jax.shard_map(
        on_device, mesh=mesh, in_specs=in_specs, out_specs=out_specs, check_vma=False
    )
```
